32 devices in a mesh: gx: 2 (over x), gy: 4 (over y, core), gz: 4 (over z).
Axes of the slice: x: 2, y: 2, z: 4, core: 2. Of those that a mesh axis runs over, the one named last changes fastest.
Arguments:
- displacement: float32 [3, 64, 128, 512], P(None, 'gz', 'gx', 'gy'), may hold values from -6 to 6
- pressure: float32 [64, 128, 512], P('gz', 'gx', 'gy'), may hold values from -6 to 6
- zone: int32 [64, 128, 512], P('gz', 'gx', 'gy'), may hold values from 0 to 7
- perm_table: float32 [8], replicated, may hold values from 0.2 to 5
- thickness: int32 [128, 512], P('gx', 'gy'), may hold values from 1 to 64, as said below
Outputs:
- heights: float32 [64, 128, 512], P('gz', 'gx', 'gy')
- flow_residual: float32 [64, 128, 512], P('gz', 'gx', 'gy')
- mech_residual: float32 [3, 64, 128, 512], P(None, 'gz', 'gx', 'gy')
The draws below stay inside these ranges and needn't reach their ends.
Inputs may be any that keep to these rules, and one draw needn't show every extreme that they name: Every draw has a column of thickness 64; a rectangular region of the lateral plane holds thick deposit, the rest thin deposit.
All inputs are finite; a program needn't handle non-finite values.
Results may differ from the reference program's by a relative error of at most 0.00002.
Values sent between devices are 32-bit elements; how exact they have to be, the bound alone decides.
A program may use at most 64 MiB of HBM per device.

```python
import math
import jax
import jax.numpy as jnp

ZONES = 8
NZ = 64
NX = 128
NY = 512


def draw_thickness(key, part):
    keys = jax.random.split(key, 4)
    shallow = jax.random.randint(keys[0], (NX, NY), max(1, NZ // 8), NZ // 4 + 1)
    deep = jax.random.randint(keys[1], (NX, NY), 3 * NZ // 4, NZ + 1)
    row_start = jax.random.randint(keys[2], (), 0, NX - NX // 4 + 1)
    col_start = jax.random.randint(keys[3], (), 0, NY - NY // 4 + 1)
    rows = jnp.arange(NX, dtype=jnp.int32)[:, None]
    cols = jnp.arange(NY, dtype=jnp.int32)[None, :]
    inside = (rows >= row_start) & (rows < row_start + NX // 4) & (cols >= col_start) & (cols < col_start + NY // 4)
    result = jnp.where(inside, deep, shallow)
    result = result.at[row_start, col_start].set(NZ)
    return result.astype(jnp.int32)


def set_ends(entries, stream_key, least, largest):
    longest = entries.shape.index(max(entries.shape))
    spots = []
    for shift in (0, 1):
        where = [jax.random.randint(jax.random.fold_in(stream_key, axis), (), 0, length) for axis, length in enumerate(entries.shape)]
        where[longest] = (where[longest] + shift) % entries.shape[longest]
        spots.append(tuple(where))
    return entries.at[spots[0]].set(least).at[spots[1]].set(largest)


def level_of(stream_key, shape, cuts, smallest, top_value):
    loudness, own = 1.0, jax.random.fold_in(stream_key, 6)
    for dim, parts in cuts:
        draws = jnp.exp(jax.random.uniform(jax.random.fold_in(own, dim), (parts,), jnp.float32, smallest / len(cuts), top_value / len(cuts)))
        loudness = loudness * jnp.repeat(draws, shape[dim] // parts).reshape([-1 if axis == dim else 1 for axis in range(len(shape))])
    return loudness


def centred(stream_key, shape, width, reach, shards=(), held_as=jnp.bfloat16):
    entries = jax.random.normal(stream_key, shape, jnp.float32) * width
    if len(shards) > 0:
        entries = level_of(stream_key, shape, shards, -0.22, 0.18) * entries
    return jnp.clip(entries, min=-reach, max=reach).astype(held_as)


def setup_inputs(seed: int = 0) -> dict:
    key_list = jax.random.split(jax.random.key(seed), 6)
    return {
        "displacement": centred(key_list[0], (3, NZ, NX, NY), 1.0, 6.0, ((1, 4), (2, 2), (3, 4)), jnp.float32),
        "pressure": centred(key_list[1], (NZ, NX, NY), 1.0, 6.0, ((0, 4), (1, 2), (2, 4)), jnp.float32),
        "zone": set_ends(jax.random.randint(key_list[2], (NZ, NX, NY), 0, ZONES), jax.random.fold_in(key_list[2], 1), 0, ZONES - 1).astype(jnp.int32),
        "perm_table": jnp.clip(jnp.exp(jax.random.uniform(key_list[3], (ZONES,), jnp.float32, math.log(0.2), math.log(5.0))), 0.2, 5.0),
        "thickness": draw_thickness(jax.random.fold_in(key_list[5], 71), 0),
    }


def take(field, dz, dx, dy):
    return field[..., 1 + dz:field.shape[-3] - 1 + dz, 1 + dx:field.shape[-2] - 1 + dx, 1 + dy:field.shape[-1] - 1 + dy]


def padded(field):
    widths = [(0, 0)] * (field.ndim - 3) + [(1, 1)] * 3
    return jnp.pad(field, widths)


def strain_of(disp_pad):
    div = 0.5 * (take(disp_pad[0], 0, 1, 0) - take(disp_pad[0], 0, -1, 0))
    div = div + 0.5 * (take(disp_pad[1], 0, 0, 1) - take(disp_pad[1], 0, 0, -1))
    div = div + 0.5 * (take(disp_pad[2], 1, 0, 0) - take(disp_pad[2], -1, 0, 0))
    return 0.3 * jnp.tanh(div)


def stencils(disp_pad, press_pad, strain_pad, perm_pad):
    press_mid = take(press_pad, 0, 0, 0)
    perm_mid = take(perm_pad, 0, 0, 0)
    strain_mid = take(strain_pad, 0, 0, 0)
    height_mid = 1.0 + strain_mid
    flow = jnp.zeros_like(press_mid)
    for dz, dx, dy in ((1, 0, 0), (-1, 0, 0), (0, 1, 0), (0, -1, 0), (0, 0, 1), (0, 0, -1)):
        perm_nb = take(perm_pad, dz, dx, dy)
        if dz == 0:
            cond = 2.0 * perm_mid * perm_nb / (perm_mid + perm_nb)
        else:
            height_nb = 1.0 + take(strain_pad, dz, dx, dy)
            cond = 4.0 * perm_mid * perm_nb / ((perm_mid + perm_nb) * (height_mid + height_nb))
        flow = flow + cond * (take(press_pad, dz, dx, dy) - press_mid)
    flow = flow - strain_mid
    disp_mid = take(disp_pad, 0, 0, 0)
    lateral = take(disp_pad, 0, 1, 0) + take(disp_pad, 0, -1, 0) + take(disp_pad, 0, 0, 1) + take(disp_pad, 0, 0, -1) - 4.0 * disp_mid
    height_up = 1.0 + take(strain_pad, 1, 0, 0)
    height_dn = 1.0 + take(strain_pad, -1, 0, 0)
    vertical = 2.0 * (take(disp_pad, 1, 0, 0) - disp_mid) / (height_mid + height_up) - 2.0 * (disp_mid - take(disp_pad, -1, 0, 0)) / (height_mid + height_dn)

    def grads(field):
        return jnp.stack([0.5 * (take(field, 0, 1, 0) - take(field, 0, -1, 0)), 0.5 * (take(field, 0, 0, 1) - take(field, 0, 0, -1)), 0.5 * (take(field, 1, 0, 0) - take(field, -1, 0, 0))])

    mech = lateral + vertical + 0.5 * grads(strain_pad) - grads(press_pad)
    return flow, mech


def reference(displacement, pressure, zone, perm_table, thickness):
    disp_pad = padded(displacement)
    strain = strain_of(disp_pad)
    layer = jnp.arange(NZ, dtype=jnp.int32)[:, None, None]
    active = (layer < thickness[None, :, :]).astype(jnp.float32)
    cell_thick = (1.0 + strain) * active
    prefix = jnp.cumsum(cell_thick, axis=0)
    heights = prefix / NZ
    burden = (prefix[-1][None, :, :] - prefix) / NZ
    zone_perm = jnp.zeros_like(strain)
    for index in range(ZONES):
        zone_perm = zone_perm + jnp.where(zone == index, perm_table[index], jnp.float32(0.0))
    kperm = zone_perm * (1.0 + strain) ** 3 / (1.0 + 2.0 * burden) * (0.001 + 0.999 * active)
    flow, mech = stencils(disp_pad, padded(pressure), padded(strain), padded(kperm))
    return heights, flow, mech
```

```python
import functools

import jax
import jax.numpy as jnp
from jax import lax
from jax.experimental import pallas as pl
from jax.experimental.pallas import tpu as pltpu
from jax.sharding import PartitionSpec as P

MESH = pl.DeviceIdType.MESH
ZONES = 8
AXES = ("gx", "gy", "gz")
PAD = 8
ROWS = 32
UNROLL = 16

X0, Y0, X1, Y1, ZU, ZL, ZP, ZN, X2, Y2, ZS, X3, Y3 = range(13)
MESSAGES = 13


def kernel(
    counts, disp, press, zone, table, thick, heights, flow, mech, lane_sides, row_sides,
    u, p, s, k, zn, th, pre, tot, xs1, xr1, ys1, yr1, ysr, yrr, xs2, xr2, ys2, yr2, xs3, xr3, ys3, yr3, cs,
    tab, load_sem, send_sem, recv_sem, col_send, col_recv,
):
    depth, width = disp.shape[1], disp.shape[2]
    lanes = disp.shape[3]
    groups = width // 8
    last = PAD + width
    me = {axis: lax.axis_index(axis) for axis in AXES}
    size = dict(zip(AXES, counts))
    depth_total = depth * size["gz"]
    own = pl.ds(PAD, width)
    f32 = jnp.float32

    def has(axis, side):
        return me[axis] > 0 if side == 0 else me[axis] < size[axis] - 1

    def peer(axis, side):
        return {axis: me[axis] + (1 if side else -1)}

    loads = [
        pltpu.make_async_copy(disp.at[1], u.at[1, pl.ds(1, depth), own], load_sem.at[0]),
        pltpu.make_async_copy(disp.at[0], u.at[0, pl.ds(1, depth), own], load_sem.at[1]),
        pltpu.make_async_copy(disp.at[2], u.at[2, pl.ds(1, depth), own], load_sem.at[2]),
        pltpu.make_async_copy(press, p.at[pl.ds(1, depth), own], load_sem.at[3]),
        pltpu.make_async_copy(thick, th, load_sem.at[4]),
        pltpu.make_async_copy(zone, zn.at[pl.ds(1, depth)], load_sem.at[5]),
        pltpu.make_async_copy(table, tab, load_sem.at[6]),
    ]
    for load in loads:
        load.start()

    barrier = pltpu.get_barrier_semaphore()
    partners = jnp.int32(size["gz"] - 1)
    for axis in ("gx", "gy"):
        for side in (0, 1):
            @pl.when(has(axis, side))
            def _():
                pl.semaphore_signal(barrier, inc=1, device_id=peer(axis, side), device_id_type=MESH)
            partners = partners + has(axis, side).astype(jnp.int32)
    for off in range(1, size["gz"]):
        pl.semaphore_signal(
            barrier, inc=1, device_id={"gz": lax.rem(me["gz"] + off, size["gz"])}, device_id_type=MESH
        )

    pending = []

    def copy(message, axis, side, src, dst, at):
        return pltpu.make_async_remote_copy(
            src_ref=src,
            dst_ref=dst,
            send_sem=send_sem.at[message, side],
            recv_sem=recv_sem.at[message, side],
            device_id=peer(axis, at),
            device_id_type=MESH,
        )

    def send(message, axis, srcs, dsts):
        for side in (0, 1):
            @pl.when(has(axis, side))
            def _():
                copy(message, axis, side, srcs[side], dsts[1 - side], side).start()
        pending.append((message, axis, srcs, dsts))

    def receive(message, axis, srcs, dsts):
        for side in (0, 1):
            @pl.when(has(axis, 1 - side))
            def _():
                copy(message, axis, side, srcs[side], dsts[1 - side], 1 - side).wait_recv()

    def clear(axis, refs):
        for side in (0, 1):
            @pl.when(jnp.logical_not(has(axis, side)))
            def _():
                for ref in refs[side]:
                    ref[...] = jnp.zeros(ref.shape, ref.dtype)

    def pair(ref):
        return (ref.at[0], ref.at[1])

    zu = ((disp.at[2, 0], disp.at[2, depth - 1]), (u.at[2, 0, own], u.at[2, depth + 1, own]))
    zl = (
        (disp.at[pl.ds(0, 2), 0], disp.at[pl.ds(0, 2), depth - 1]),
        (u.at[pl.ds(0, 2), 0, own], u.at[pl.ds(0, 2), depth + 1, own]),
    )
    zp = ((press.at[0], press.at[depth - 1]), (p.at[0, own], p.at[depth + 1, own]))
    zz = ((zone.at[0], zone.at[depth - 1]), (zn.at[0], zn.at[depth + 1]))
    zs = ((s.at[1, own], s.at[depth, own]), (s.at[0, own], s.at[depth + 1, own]))
    lane = lax.broadcasted_iota(jnp.int32, (8, lanes), 1)
    lane_r = lax.broadcasted_iota(jnp.int32, (ROWS, lanes), 1)
    first_lane, last_lane = lane_r == 0, lane_r == lanes - 1
    zero8 = jnp.zeros((8, lanes), f32)

    def pack(values, z, g, lo, hi):
        slot = z * groups + g
        turned = pltpu.roll(values, slot, 1)
        hi = jnp.where(lane == slot, turned, hi)
        lo = jnp.where(lane == lax.rem(slot + lanes - 1, lanes), turned, lo)
        return lo, hi

    def yshift(v, packs, z, row):
        if packs is None:
            below = jnp.where(first_lane, 0.0, pltpu.roll(v, 1, 1))
            return below, jnp.where(last_lane, 0.0, pltpu.roll(v, lanes - 1, 1))
        lo, hi = [], []
        lo_pack, hi_pack = packs
        for g in range(ROWS // 8):
            slot = z * groups + row // 8 + g
            lo.append(pltpu.roll(lo_pack, lax.rem(lanes + 1 - slot, lanes), 1))
            hi.append(pltpu.roll(hi_pack, lanes - 1 - slot, 1))
        lo, hi = jnp.concatenate(lo, axis=0), jnp.concatenate(hi, axis=0)
        below = jnp.where(first_lane, lo, pltpu.roll(v, 1, 1))
        above = jnp.where(last_lane, hi, pltpu.roll(v, lanes - 1, 1))
        return below, above

    fields = [u.at[0], u.at[1], u.at[2], p]

    def pack_first(z, carry):
        lo, hi = carry
        xs1[0, 0, z] = u[0, z + 1, PAD:PAD + 1, :]
        xs1[1, 0, z] = u[0, z + 1, last - 1:last, :]
        for g in range(groups):
            lo, hi = pack(u[1, z + 1, PAD + 8 * g:PAD + 8 * g + 8, :], z, g, lo, hi)
        return lo, hi

    loads[0].wait()
    loads[1].wait()
    lo, hi = lax.fori_loop(0, depth, pack_first, (zero8,) * 2, unroll=UNROLL)
    ys1[0] = hi
    ys1[1] = lo

    def part(ref, which):
        return (ref.at[0, which], ref.at[1, which])

    x0, y0 = (part(xs1, 0), part(xr1, 0)), (pair(ys1), pair(yr1))
    x1, y1 = (part(xs1, pl.ds(1, 3)), part(xr1, pl.ds(1, 3))), (pair(ysr), pair(yrr))
    pl.semaphore_wait(barrier, partners)
    send(ZU, "gz", *zu)
    send(X0, "gx", *x0)
    send(Y0, "gy", *y0)

    others = ((0, 0), (2, 1), (3, 2))

    def pack_inputs(z, accs):
        out = []
        for i in range(1, 4):
            xs1[0, i, z] = fields[i][z + 1, PAD:PAD + 1, :]
            xs1[1, i, z] = fields[i][z + 1, last - 1:last, :]
        for i, n in others:
            lo, hi = accs[2 * n:2 * n + 2]
            for g in range(groups):
                lo, hi = pack(fields[i][z + 1, PAD + 8 * g:PAD + 8 * g + 8, :], z, g, lo, hi)
            out += [lo, hi]
        return tuple(out)

    loads[2].wait()
    loads[3].wait()
    accs = lax.fori_loop(0, depth, pack_inputs, (zero8,) * 6, unroll=UNROLL)
    for i, n in others:
        ysr[0, n] = accs[2 * n + 1]
        ysr[1, n] = accs[2 * n]
    x2, y2 = (pair(xs2), pair(xr2)), (pair(ys2), pair(yr2))
    x3, y3 = (pair(xs3), pair(xr3)), (pair(ys3), pair(yr3))
    send(X1, "gx", *x1)
    send(Y1, "gy", *y1)
    send(ZL, "gz", *zl)
    send(ZP, "gz", *zp)
    send(ZN, "gz", *zz)

    clear("gx", [[xr.at[side] for xr in (xr1, xr2, xr3)] for side in (0, 1)])
    clear("gy", [[yr.at[side] for yr in (yr1, yrr, yr2, yr3)] for side in (0, 1)])
    edges = (0, depth + 1)
    clear("gz", [[u.at[:, z, own], p.at[z, own], s.at[z, own], k.at[z, own], zn.at[z]] for z in edges])
    loads[4].wait()

    receive(ZU, "gz", *zu)
    receive(X0, "gx", *x0)
    receive(Y0, "gy", *y0)

    def unpack_first(z, carry):
        u[0, z + 1, PAD - 1:PAD, :] = xr1[0, 0, z]
        u[0, z + 1, last:last + 1, :] = xr1[1, 0, z]
        return carry

    lax.fori_loop(0, depth, unpack_first, 0, unroll=UNROLL)

    def unpack_inputs(z, carry):
        for i in range(1, 4):
            fields[i][z + 1, PAD - 1:PAD, :] = xr1[0, i, z]
            fields[i][z + 1, last:last + 1, :] = xr1[1, i, z]
        k[z + 1, PAD - 1:PAD, :] = jnp.zeros((1, lanes), f32)
        k[z + 1, last:last + 1, :] = jnp.zeros((1, lanes), f32)
        return carry

    def shifts(field, packs, z, row):
        at = PAD + row
        mid = field[z + 1, at:at + ROWS, :]
        xm = field[z + 1, at - 1:at - 1 + ROWS, :]
        xp = field[z + 1, at + 1:at + 1 + ROWS, :]
        ym, yp = yshift(mid, packs, z, row)
        return mid, xm, xp, ym, yp

    base = me["gz"] * depth
    chunks = range(0, width, ROWS)

    ylo, yhi = zero8, zero8
    for row in chunks:
        rows = slice(row, row + ROWS)
        at = slice(PAD + row, PAD + row + ROWS)
        height = th[rows, :]
        packs = (yr1[0], yr1[1])

        def strain_step(z, carry):
            acc, lo, hi = carry
            up = u[0, z + 1, PAD + row + 1:PAD + row + 1 + ROWS, :]
            down = u[0, z + 1, PAD + row - 1:PAD + row - 1 + ROWS, :]
            ym, yp = yshift(u[1, z + 1, at, :], packs, z, row)
            div = 0.5 * (up - down) + 0.5 * (yp - ym) + 0.5 * (u[2, z + 2, at, :] - u[2, z, at, :])
            st = 0.3 * jnp.tanh(div)
            s[z + 1, at, :] = st
            if row == 0:
                xs2[0, z] = st[0:1, :]
            if row + ROWS == width:
                xs2[1, z] = st[ROWS - 1:ROWS, :]
            for g in range(ROWS // 8):
                lo, hi = pack(st[8 * g:8 * g + 8, :], z, row // 8 + g, lo, hi)
            acc = acc + jnp.where(base + z < height, 1.0 + st, 0.0)
            pre[z, rows, :] = acc
            return acc, lo, hi

        acc, ylo, yhi = lax.fori_loop(0, depth, strain_step, (jnp.zeros((ROWS, lanes), f32), ylo, yhi), unroll=UNROLL)
        tot[rows, :] = acc
    ys2[0], ys2[1] = yhi, ylo

    def column(off, at):
        return pltpu.make_async_remote_copy(
            src_ref=tot,
            dst_ref=cs.at[off - 1],
            send_sem=col_send.at[off - 1],
            recv_sem=col_recv.at[off - 1],
            device_id={"gz": lax.rem(me["gz"] + at, size["gz"])},
            device_id_type=MESH,
        )

    for off in range(1, size["gz"]):
        column(off, off).start()
    send(X2, "gx", *x2)
    send(Y2, "gy", *y2)
    send(ZS, "gz", *zs)

    receive(ZP, "gz", *zp)
    receive(X1, "gx", *x1)
    receive(Y1, "gy", *y1)
    lax.fori_loop(0, depth, unpack_inputs, 0, unroll=UNROLL)
    for row in chunks:
        rows = slice(row, row + ROWS)
        at = slice(PAD + row, PAD + row + ROWS)
        packs = [(yrr[0, 0], yrr[1, 0]), (yr1[0], yr1[1]), (yrr[0, 1], yrr[1, 1]), (yrr[0, 2], yrr[1, 2])]

        def lateral_step(z, carry):
            _, xm, xp, ym, yp = shifts(p, packs[3], z, row)
            grads = (xp - xm, yp - ym, p[z + 2, at, :] - p[z, at, :])
            for c in range(3):
                mid, xm, xp, ym, yp = shifts(u.at[c], packs[c], z, row)
                mech[c, z, rows, :] = xp + xm + yp + ym - 4.0 * mid - 0.5 * grads[c]
            return carry

        lax.fori_loop(0, depth, lateral_step, 0, unroll=UNROLL)

    loads[5].wait()
    loads[6].wait()

    def unloaded(zones, st, active):
        h = 1.0 + st
        perm = jnp.full(zones.shape, tab[0], f32)
        for i in range(1, ZONES):
            perm = jnp.where(zones == i, tab[i], perm)
        return perm * (h * h * h) * jnp.where(active, 0.001 + 0.999, 0.001)

    for row in chunks:
        rows = slice(row, row + ROWS)
        at = slice(PAD + row, PAD + row + ROWS)
        height = th[rows, :]

        def unloaded_step(z, carry):
            k[z + 1, at, :] = unloaded(zn[z + 1, rows, :], s[z + 1, at, :], base + z < height)
            return carry

        lax.fori_loop(0, depth, unloaded_step, 0, unroll=UNROLL)

    for off in range(1, size["gz"]):
        column(off, size["gz"] - off).wait_recv()

    def column_ends(rows):
        offset = jnp.zeros((ROWS, lanes), f32)
        total = tot[rows, :]
        for off in range(1, size["gz"]):
            piece = cs[off - 1, rows, :]
            offset = offset + piece * (me["gz"] >= off).astype(f32)
            total = total + piece
        return offset, total

    def permeability(free, burden):
        return free / (1.0 + 2.0 * burden)

    ylo, yhi = zero8, zero8
    for row in chunks:
        rows = slice(row, row + ROWS)
        at = slice(PAD + row, PAD + row + ROWS)
        offset, total = column_ends(rows)

        def kperm_step(z, carry):
            lo, hi = carry
            prefix = pre[z, rows, :] + offset
            heights[z, rows, :] = prefix / depth_total
            kp = permeability(k[z + 1, at, :], (total - prefix) / depth_total)
            k[z + 1, at, :] = kp
            if row == 0:
                xs3[0, z] = kp[0:1, :]
            if row + ROWS == width:
                xs3[1, z] = kp[ROWS - 1:ROWS, :]
            for g in range(ROWS // 8):
                lo, hi = pack(kp[8 * g:8 * g + 8, :], z, row // 8 + g, lo, hi)
            return lo, hi

        ylo, yhi = lax.fori_loop(0, depth, kperm_step, (ylo, yhi), unroll=UNROLL)

    ys3[0], ys3[1] = yhi, ylo
    send(X3, "gx", *x3)
    send(Y3, "gy", *y3)

    receive(ZS, "gz", *zs)
    receive(ZN, "gz", *zz)
    for row in chunks:
        rows = slice(row, row + ROWS)
        at = slice(PAD + row, PAD + row + ROWS)
        height = th[rows, :]
        offset, total = column_ends(rows)

        @pl.when(has("gz", 0))
        def _():
            free = unloaded(zn[0, rows, :], s[0, at, :], base - 1 < height)
            k[0, at, :] = permeability(free, (total - offset) / depth_total)

        @pl.when(has("gz", 1))
        def _():
            st = s[depth + 1, at, :]
            active = base + depth < height
            prefix = offset + tot[rows, :] + jnp.where(active, 1.0 + st, 0.0)
            free = unloaded(zn[depth + 1, rows, :], st, active)
            k[depth + 1, at, :] = permeability(free, (total - prefix) / depth_total)

    for row in chunks:
        rows = slice(row, row + ROWS)

        def flow_step(z, carry):
            ka, *ks = shifts(k, None, z, row)
            pa, *ps = shifts(p, None, z, row)
            out = jnp.zeros((ROWS, lanes), f32)
            twice = 2.0 * ka
            for kb, pb in zip(ks, ps):
                out = out + twice * kb / (ka + kb) * (pb - pa)
            flow[z, rows, :] = out
            return carry

        lax.fori_loop(0, depth, flow_step, 0, unroll=UNROLL)

    receive(ZL, "gz", *zl)
    receive(X2, "gx", *x2)
    receive(Y2, "gy", *y2)

    def unpack_strain(z, carry):
        s[z + 1, PAD - 1:PAD, :] = xr2[0, z]
        s[z + 1, last:last + 1, :] = xr2[1, z]
        return carry

    lax.fori_loop(0, depth, unpack_strain, 0, unroll=UNROLL)

    for row in chunks:
        rows = slice(row, row + ROWS)
        at = slice(PAD + row, PAD + row + ROWS)
        packs = (yr2[0], yr2[1])

        def faces(z):
            ka, kb = k[z, at, :], k[z + 1, at, :]
            hh = 2.0 + s[z, at, :] + s[z + 1, at, :]
            twice = 2.0 / hh
            cond = 2.0 * twice * (ka * kb) / (ka + kb)
            fluxes = [twice * (u[c, z + 1, at, :] - u[c, z, at, :]) for c in range(3)]
            return fluxes, cond * (p[z + 1, at, :] - p[z, at, :])

        def vertical_step(z, carry):
            below, flow_below = carry
            above, flow_above = faces(z + 1)
            mid, xm, xp, ym, yp = shifts(s, packs, z, row)
            flow[z, rows, :] = flow[z, rows, :] + (flow_above - flow_below) - mid
            grads = (xp - xm, yp - ym, s[z + 2, at, :] - s[z, at, :])
            for c in range(3):
                mech[c, z, rows, :] = mech[c, z, rows, :] + (above[c] - below[c]) + 0.25 * grads[c]
            return above, flow_above

        lax.fori_loop(0, depth, vertical_step, faces(0), unroll=UNROLL)

    receive(X3, "gx", *x3)
    receive(Y3, "gy", *y3)

    def crossing(ka, kb, pa, pb):
        return 2.0 * ka * kb / (ka + kb) * (pb - pa)

    turn = lambda face: pltpu.roll(face, 1, 1)
    lane_sides[0] = crossing(ys3[0], turn(yr3[0]), ysr[0, 2], turn(yrr[0, 2]))
    lane_sides[1] = crossing(turn(ys3[1]), yr3[1], turn(ysr[1, 2]), yrr[1, 2])

    def sides_step(z, carry):
        for side in (0, 1):
            row_sides[side, z] = crossing(xs3[side, z], xr3[side, z], xs1[side, 3, z], xr1[side, 3, z])
        return carry

    lax.fori_loop(0, depth, sides_step, 0, unroll=UNROLL)

    for message, axis, srcs, dsts in pending:
        for side in (0, 1):
            @pl.when(has(axis, side))
            def _():
                copy(message, axis, side, srcs[side], dsts[1 - side], side).wait_send()
    for off in range(1, size["gz"]):
        column(off, off).wait_send()


def store(heights, flow, mech, lane_sides, row_sides, heights_out, flow_out, mech_out, whole, sem):
    depth, width, lanes = whole.shape
    groups = width // 8
    copies = [
        pltpu.make_async_copy(mech, mech_out, sem.at[0]),
        pltpu.make_async_copy(heights, heights_out, sem.at[1]),
    ]
    for copy in copies:
        copy.start()
    lane = lax.broadcasted_iota(jnp.int32, (8, lanes), 1)
    first, last = lane == 0, lane == lanes - 1
    side_lo, side_hi = lane_sides[0], lane_sides[1]

    def step(z, carry):
        for g in range(groups):
            slot = z * groups + g
            lo = pltpu.roll(side_lo, lax.rem(lanes - slot, lanes), 1)
            hi = pltpu.roll(side_hi, lanes - 1 - slot, 1)
            rows = slice(8 * g, 8 * g + 8)
            whole[z, rows, :] = flow[z, rows, :] + jnp.where(first, lo, jnp.where(last, hi, 0.0))
        for side, row in ((0, 0), (1, width - 1)):
            whole[z, row:row + 1, :] = whole[z, row:row + 1, :] + row_sides[side, z]
        return carry

    half = depth // 2
    for part in range(2):
        lax.fori_loop(part * half, (part + 1) * half, step, 0, unroll=4)
        layers = pl.ds(part * half, half)
        copy = pltpu.make_async_copy(whole.at[layers], flow_out.at[layers], sem.at[2 + part])
        copy.start()
        copies.append(copy)
    for copy in copies:
        copy.wait()


def local(counts, displacement, pressure, zone, perm_table, thickness):
    _, depth, width, lanes = displacement.shape
    f32 = jnp.float32
    tall = (depth + 2, width + 2 * PAD, lanes)
    row_face = lambda *lead: pltpu.VMEM((2, *lead, depth, 1, lanes), f32)
    lane_face = lambda *lead: pltpu.VMEM((2, *lead, 8, lanes), f32)
    hbm, vmem = (pl.BlockSpec(memory_space=m) for m in (pl.ANY, pltpu.VMEM))
    others = max(counts[2] - 1, 1)
    inputs = [
        pltpu.with_memory_space_constraint(x, pltpu.HBM)
        for x in (displacement, pressure, zone, perm_table, thickness)
    ]
    fields = pl.pallas_call(
        functools.partial(kernel, counts),
        out_shape=(
            pltpu.VMEM(pressure.shape, f32),
            pltpu.VMEM(pressure.shape, f32),
            pltpu.VMEM(displacement.shape, f32),
            pltpu.VMEM((2, 8, lanes), f32),
            pltpu.VMEM((2, depth, 1, lanes), f32),
        ),
        in_specs=[hbm] * 5,
        out_specs=(vmem,) * 5,
        scratch_shapes=[
            pltpu.VMEM((3, *tall), f32),
            pltpu.VMEM(tall, f32),
            pltpu.VMEM(tall, f32),
            pltpu.VMEM(tall, f32),
            pltpu.VMEM((depth + 2, width, lanes), jnp.int32),
            pltpu.VMEM((width, lanes), jnp.int32),
            pltpu.VMEM((depth, width, lanes), f32),
            pltpu.VMEM((width, lanes), f32),
            row_face(4), row_face(4), lane_face(), lane_face(), lane_face(3), lane_face(3),
            row_face(), row_face(), lane_face(), lane_face(),
            row_face(), row_face(), lane_face(), lane_face(),
            pltpu.VMEM((others, width, lanes), f32),
            pltpu.SMEM((ZONES,), f32),
            pltpu.SemaphoreType.DMA((7,)),
            pltpu.SemaphoreType.DMA((MESSAGES, 2)),
            pltpu.SemaphoreType.DMA((MESSAGES, 2)),
            pltpu.SemaphoreType.DMA((others,)),
            pltpu.SemaphoreType.DMA((others,)),
        ],
        compiler_params=pltpu.CompilerParams(
            collective_id=0, has_side_effects=True, vmem_limit_bytes=40 * 2**20
        ),
    )(*inputs)
    return pl.pallas_call(
        store,
        out_shape=tuple(jax.ShapeDtypeStruct(x.shape, f32) for x in (pressure, pressure, displacement)),
        in_specs=[vmem] * 5,
        out_specs=(hbm,) * 3,
        scratch_shapes=[pltpu.VMEM(pressure.shape, f32), pltpu.SemaphoreType.DMA((4,))],
        compiler_params=pltpu.CompilerParams(vmem_limit_bytes=4 * 2**20),
    )(*[pltpu.with_memory_space_constraint(x, pltpu.VMEM) for x in fields])


def solution(mesh):
    counts = tuple(mesh.shape[axis] for axis in AXES)
    in_specs = (
        P(None, "gz", "gx", "gy"),
        P("gz", "gx", "gy"),
        P("gz", "gx", "gy"),
        P(),
        P("gx", "gy"),
    )
    out_specs = (P("gz", "gx", "gy"), P("gz", "gx", "gy"), P(None, "gz", "gx", "gy"))
    return jax.shard_map(
        functools.partial(local, counts), mesh=mesh, in_specs=in_specs, out_specs=out_specs, check_vma=False
    )
```

```python
import functools

import jax
import jax.numpy as jnp
from jax import lax
from jax.experimental import pallas as pl
from jax.experimental.pallas import tpu as pltpu
from jax.sharding import PartitionSpec as P

MESH = pl.DeviceIdType.MESH
ZONES = 8
AXES = ("gx", "gy", "gz")
PAD = 8
ROWS = 32

ZU, ZB, X0, Y0, X1, Y1, ZS, X2, Y2 = range(9)


def kernel(
    counts, disp, press, zone, table, thick,
    pre, off_out, r, gx, gy, gz, s, mech, flow_sides, mech_sides, row_sides,
    u, p, t, zn, th, tab, ip, inv, tot, tail,
    xs, xr, ys, yr, xe, xer, ye, yer, zr, zp, tx, txr, ty, tyr, cs,
    load_sem, recv_sem, side_send, col_send, col_recv, edge_send, edge_recv,
):
    depth, width, lanes = press.shape
    groups = width // 8
    last = PAD + width
    me = {axis: lax.axis_index(axis) for axis in AXES}
    size = dict(zip(AXES, counts))
    depth_total = depth * size["gz"]
    scale = 2.0 / depth_total
    own = pl.ds(PAD, width)
    f32 = jnp.float32
    chunks = range(0, width, ROWS)
    far = range(1, size["gz"])

    def has(axis, side):
        return me[axis] > 0 if side == 0 else me[axis] < size[axis] - 1

    def mask(axis, side):
        return has(axis, side).astype(f32)

    def peer(axis, side, up=0):
        place = {axis: me[axis] + (1 if side else -1)}
        if up:
            place["gz"] = me["gz"] + up
        return place

    def round_z(off):
        return {"gz": lax.rem(me["gz"] + off, size["gz"])}

    def both(axis, side, off):
        inside = me["gz"] + off < size["gz"] if off > 0 else me["gz"] + off >= 0
        return jnp.logical_and(has(axis, side), inside)

    def loop(step, carry, start=0, end=depth):
        return lax.fori_loop(start, end, step, carry, unroll=end - start)

    inner = pl.ds(1, depth)
    loads = [
        pltpu.make_async_copy(disp.at[1], u.at[1, inner, own], load_sem.at[0]),
        pltpu.make_async_copy(disp.at[0], u.at[0, inner, own], load_sem.at[1]),
        pltpu.make_async_copy(disp.at[2], u.at[2, inner, own], load_sem.at[2]),
        pltpu.make_async_copy(press, p.at[inner, own], load_sem.at[3]),
        pltpu.make_async_copy(zone, zn.at[inner], load_sem.at[4]),
        pltpu.make_async_copy(thick, th, load_sem.at[5]),
        pltpu.make_async_copy(table, tab, load_sem.at[6]),
    ]
    for load in loads:
        load.start()

    barrier = pltpu.get_barrier_semaphore()
    partners = jnp.int32(size["gz"] - 1)
    for axis in ("gx", "gy"):
        for side in (0, 1):
            @pl.when(has(axis, side))
            def _():
                pl.semaphore_signal(barrier, inc=1, device_id=peer(axis, side), device_id_type=MESH)
            for off in far:
                @pl.when(both(axis, side, off))
                def _():
                    pl.semaphore_signal(barrier, inc=1, device_id=peer(axis, side, off), device_id_type=MESH)
            partners = partners + has(axis, side).astype(jnp.int32) * (1 + me["gz"])
    for off in far:
        pl.semaphore_signal(barrier, inc=1, device_id=round_z(off), device_id_type=MESH)

    def copy(message, axis, side, src, dst, at):
        return pltpu.make_async_remote_copy(
            src_ref=src,
            dst_ref=dst,
            send_sem=side_send.at[AXES.index(axis), side],
            recv_sem=recv_sem.at[message, side],
            device_id=peer(axis, at),
            device_id_type=MESH,
        )

    def send(message, axis, *parts):
        for side in (0, 1):
            @pl.when(has(axis, side))
            def _():
                for srcs, dsts in parts:
                    copy(message, axis, side, srcs[side], dsts[1 - side], side).start()

    def receive(message, axis, whole):
        for side in (0, 1):
            @pl.when(has(axis, side))
            def _():
                pltpu.make_async_copy(whole, whole, recv_sem.at[message, 1 - side]).wait()

    def clear(axis, refs):
        for side in (0, 1):
            @pl.when(jnp.logical_not(has(axis, side)))
            def _():
                for ref in refs[side]:
                    ref[...] = jnp.zeros(ref.shape, ref.dtype)

    def pair(ref, *at):
        return (ref.at[(0, *at)], ref.at[(1, *at)])

    zu = ((disp.at[2, 0], disp.at[2, depth - 1]), (u.at[2, 0, own], u.at[2, depth + 1, own]))
    zl = (
        (disp.at[pl.ds(0, 2), 0], disp.at[pl.ds(0, 2), depth - 1]),
        (u.at[pl.ds(0, 2), 0, own], u.at[pl.ds(0, 2), depth + 1, own]),
    )
    zq = ((press.at[0], press.at[depth - 1]), (p.at[0, own], p.at[depth + 1, own]))
    zz = ((zone.at[0], zone.at[depth - 1]), (zn.at[0], zn.at[depth + 1]))
    zs = ((s.at[1], s.at[depth]), (s.at[0], s.at[depth + 1]))
    x0, y0 = (pair(xs, 0), pair(xr, 0)), (pair(ys, 0), pair(yr, 0))
    x1, y1 = (pair(xs, pl.ds(1, 3)), pair(xr, pl.ds(1, 3))), (pair(ys, pl.ds(1, 3)), pair(yr, pl.ds(1, 3)))
    x2, y2 = (pair(xe), pair(xer)), (pair(ye), pair(yer))

    lane = lax.broadcasted_iota(jnp.int32, (8, lanes), 1)
    odd = lax.rem(lane, 2) == 1
    lane_r = lax.broadcasted_iota(jnp.int32, (ROWS, lanes), 1)
    first_lane, last_lane = lane_r == 0, lane_r == lanes - 1
    zero8 = jnp.zeros((8, lanes), f32)

    def pack(values, slot, packs):
        turned = pltpu.roll(values, slot, 1)
        low = jnp.where(lane == slot, turned, packs[0])
        return low, jnp.where(lane == lax.rem(slot + lanes - 1, lanes), turned, packs[1])

    def keep(ref, packs, *at):
        ref[(0, *at)] = packs[0]
        ref[(1, *at)] = pltpu.roll(packs[1], 1, 1)

    def pack_rows(values, z, row, packs):
        for g in range(values.shape[0] // 8):
            packs = pack(values[8 * g:8 * g + 8, :], z * groups + row // 8 + g, packs)
        return packs

    def weave(low, high):
        low = pltpu.roll(low, 1, 1)
        return jnp.where(odd, low, high), jnp.where(odd, high, low)

    def ends_at(woven, z, row):
        parts = []
        for g in range(ROWS // 8):
            slot = z * groups + row // 8 + g
            parts.append(pltpu.roll(woven[(row // 8 + g) % 2], lanes - 1 - slot, 1))
        return jnp.concatenate(parts, axis=0)

    def yshift(v, ends):
        below, above = pltpu.roll(v, 1, 1), pltpu.roll(v, lanes - 1, 1)
        return jnp.where(first_lane, ends, below), jnp.where(last_lane, ends, above)

    fields = [u.at[0], u.at[1], u.at[2], p]

    def pack_field(i, n):
        def step(z, packs):
            return pack_rows(fields[i][z + 1, PAD:last, :], z, 0, packs)

        keep(ys, loop(step, (zero8, zero8)), n)

    def take_rows(i):
        def step(z, carry):
            xs[0, i, pl.ds(z, 1), :] = fields[i][z + 1, PAD:PAD + 1, :]
            xs[1, i, pl.ds(z, 1), :] = fields[i][z + 1, last - 1:last, :]
            return carry

        loop(step, 0)

    loads[0].wait()
    pack_field(1, 0)
    loads[1].wait()
    take_rows(0)
    pl.semaphore_wait(barrier, partners)
    send(ZU, "gz", zu)
    send(X0, "gx", x0)
    send(Y0, "gy", y0)
    send(ZB, "gz", zl, zq, zz)

    loads[2].wait()
    loads[3].wait()
    for i in range(1, 4):
        take_rows(i)
    pack_field(0, 1)
    pack_field(2, 2)
    pack_field(3, 3)
    send(X1, "gx", x1)
    send(Y1, "gy", y1)

    clear("gx", [[ref.at[side] for ref in (xr, xer)] for side in (0, 1)])
    clear("gy", [[ref.at[side] for ref in (yr, yer)] for side in (0, 1)])
    edges = (0, depth + 1)
    clear("gz", [[u.at[:, z, own], p.at[z, own], s.at[z], zn.at[z]] for z in edges])
    for axis, ref in (("gx", txr), ("gy", tyr)):
        for side in (0, 1):
            for off in far:
                @pl.when(jnp.logical_not(both(axis, side, off)))
                def _():
                    ref[side, off - 1] = jnp.zeros(ref.shape[2:], f32)

    for load in loads[4:]:
        load.wait()
    base = me["gz"] * depth

    inverse = [1.0 / jnp.full((8, lanes), tab[i], f32) for i in range(ZONES)]

    def rows_resistance(zones, active):
        count = zones.shape[0] // 8
        least = jnp.concatenate([inverse[0]] * count, axis=0)
        for i in range(1, ZONES):
            least = jnp.where(zones == i, jnp.concatenate([inverse[i]] * count, axis=0), least)
        return jnp.where(active, least * (1.0 / (0.001 + 0.999)), least * (1.0 / 0.001))

    def zone_step(z, packs):
        for row in chunks:
            zones = zn[z + 1, row:row + ROWS, :]
            ip[z, row:row + ROWS, :] = rows_resistance(zones, base + z < th[row:row + ROWS, :])
            packs = pack_rows(zones, z, row, packs)
        zr[0, pl.ds(z, 1), :] = zn[z + 1, 0:1, :]
        zr[1, pl.ds(z, 1), :] = zn[z + 1, width - 1:width, :]
        return packs

    none8 = jnp.zeros((8, lanes), jnp.int32)
    keep(zp, loop(zone_step, (none8, none8)))

    def spread(packs):
        low, high = packs[0], pltpu.roll(packs[1], 1, 1)
        step = groups
        while step < lanes:
            low, high = low + pltpu.roll(low, step, 1), high + pltpu.roll(high, step, 1)
            step *= 2
        return low, high

    edge_height = spread(pack_rows(th[...], 0, 0, (none8, none8)))
    edge_layer = base + lane // groups

    receive(ZU, "gz", zu[1][0])
    receive(X0, "gx", xr.at[0, 0])
    receive(Y0, "gy", yr.at[0, 0])

    def unpack_first(z, carry):
        u[0, z + 1, PAD - 1:PAD, :] = xr[0, 0, pl.ds(z, 1), :]
        u[0, z + 1, last:last + 1, :] = xr[1, 0, pl.ds(z, 1), :]
        return carry

    loop(unpack_first, 0)

    packs = (zero8, zero8)
    woven = weave(yr[0, 0], yr[1, 0])
    for row in chunks:
        rows = slice(row, row + ROWS)
        at = slice(PAD + row, PAD + row + ROWS)
        height = th[rows, :]

        def strain_step(z, carry):
            acc, *packs = carry
            up = u[0, z + 1, PAD + row + 1:PAD + row + 1 + ROWS, :]
            down = u[0, z + 1, PAD + row - 1:PAD + row - 1 + ROWS, :]
            ym, yp = yshift(u[1, z + 1, at, :], ends_at(woven, z, row))
            div = 0.5 * ((up - down) + (yp - ym) + (u[2, z + 2, at, :] - u[2, z, at, :]))
            st = 0.3 * jnp.tanh(div)
            s[z + 1, rows, :] = st
            t[z, at, :] = 0.25 * st - 0.5 * p[z + 1, at, :]
            if row == 0:
                xe[0, 0, pl.ds(z, 1), :] = st[0:1, :]
            if row + ROWS == width:
                xe[1, 0, pl.ds(z, 1), :] = st[ROWS - 1:ROWS, :]
            packs = pack_rows(st, z, row, packs)
            acc = acc + jnp.where(base + z < height, 1.0 + st, 0.0)
            pre[z, rows, :] = acc
            return acc, *packs

        acc, *packs = loop(strain_step, (jnp.zeros((ROWS, lanes), f32), *packs))
        tot[rows, :] = acc

    def column(off, at):
        return pltpu.make_async_remote_copy(
            src_ref=tot,
            dst_ref=cs.at[off - 1],
            send_sem=col_send.at[0],
            recv_sem=col_recv.at[off - 1],
            device_id=round_z(at),
            device_id_type=MESH,
        )

    for off in far:
        column(off, off).start()
    send(ZS, "gz", zs)

    edge = packs[0], pltpu.roll(packs[1], 1, 1)
    for side in (0, 1):
        st = edge[side]
        active = edge_layer < edge_height[side]
        thickness = jnp.where(active, 1.0 + st, 0.0)
        total, above, step = thickness, thickness, groups
        while step < lanes:
            total = total + pltpu.roll(total, step, 1)
            above = above + jnp.where(lane < lanes - step, pltpu.roll(above, lanes - step, 1), 0.0)
            step *= 2
        h = 1.0 + st
        ty[side] = total
        ye[side, 0] = st
        ye[side, 1] = 1.0 + scale * (above - thickness)
        ye[side, 2] = rows_resistance(zp[side], active) / (h * h * h)
        row = (width - 1) * side
        tx[side] = tot[row:row + 1, :]

        def row_step(z, carry):
            xe[side, 1, pl.ds(z, 1), :] = 1.0 + scale * (tot[row:row + 1, :] - pre[z, row:row + 1, :])
            return carry

        loop(row_step, 0)
        h = 1.0 + xe[side, 0]
        layer = base + lax.broadcasted_iota(jnp.int32, (depth, lanes), 0)
        xe[side, 2] = rows_resistance(zr[side], layer < th[row:row + 1, :]) / (h * h * h)

    def edge_copy(axis, side, off, at, up):
        i = ("gx", "gy").index(axis)
        src, dst = ((tx, txr), (ty, tyr))[i]
        return pltpu.make_async_remote_copy(
            src_ref=src.at[side],
            dst_ref=dst.at[1 - side, off - 1],
            send_sem=edge_send.at[i, side, off - 1],
            recv_sem=edge_recv.at[i, side, off - 1],
            device_id=peer(axis, at, up),
            device_id_type=MESH,
        )

    for off in far:
        for axis in ("gx", "gy"):
            for side in (0, 1):
                @pl.when(both(axis, side, -off))
                def _():
                    edge_copy(axis, side, off, side, -off).start()
    send(X2, "gx", x2)
    send(Y2, "gy", y2)

    receive(X1, "gx", xr.at[0, pl.ds(1, 3)])
    receive(Y1, "gy", yr.at[0, pl.ds(1, 3)])

    def unpack_inputs(z, carry):
        for side, at in ((0, PAD - 1), (1, last)):
            for i in (1, 2):
                fields[i][z + 1, at:at + 1, :] = xr[side, i, pl.ds(z, 1), :]
            t[z, at:at + 1, :] = -0.5 * xr[side, 3, pl.ds(z, 1), :]
        return carry

    loop(unpack_inputs, 0)

    wovens = [weave(yr[0, n], yr[1, n]) for n in (1, 0, 2)]
    for row in chunks:
        rows = slice(row, row + ROWS)
        at = slice(PAD + row, PAD + row + ROWS)
        up1 = slice(PAD + row + 1, PAD + row + 1 + ROWS)
        down1 = slice(PAD + row - 1, PAD + row - 1 + ROWS)
        height = tot[rows, :]

        def inner_step(z, below, bottom=False, top=False):
            mids = [u[c, z + 1, at, :] for c in range(3)]
            pm, st, tm = p[z + 1, at, :], s[z + 1, rows, :], t[z, at, :]
            above = None
            if not top:
                twice = 2.0 / (2.0 + st + s[z + 2, rows, :])
                above = [twice * (u[c, z + 2, at, :] - mids[c]) for c in range(3)]
                gz[z + 1, rows, :] = 2.0 * twice * (p[z + 2, at, :] - pm)
            tb, ta = pltpu.roll(tm, 1, 1), pltpu.roll(tm, lanes - 1, 1)
            grads = [
                t[z, up1, :] - t[z, down1, :],
                jnp.where(last_lane, 0.0, ta) - jnp.where(first_lane, 0.0, tb),
            ]
            if bottom:
                grads.append(t[z + 1, at, :])
            elif top:
                grads.append(-t[z - 1, at, :])
            else:
                grads.append(t[z + 1, at, :] - t[z - 1, at, :])
            for c in range(3):
                ym, yp = yshift(mids[c], ends_at(wovens[c], z, row))
                out = u[c, z + 1, up1, :] + u[c, z + 1, down1, :] + ym + yp - 4.0 * mids[c] + grads[c]
                if not top:
                    out = out + above[c]
                if not bottom:
                    out = out - below[c]
                mech[c, z, rows, :] = out
            gx[z, rows, :] = 2.0 * (p[z + 1, up1, :] - pm)
            gy[z, rows, :] = jnp.where(last_lane, 0.0, 2.0 * (pltpu.roll(pm, lanes - 1, 1) - pm))
            h = 1.0 + st
            free = ip[z, rows, :] / (h * h * h)
            inv[z, rows, :] = free
            r[z + 1, rows, :] = free + (scale * (height - pre[z, rows, :])) * free
            return tuple(above) if above else None

        below = inner_step(0, None, bottom=True)
        below = loop(lambda z, b: inner_step(z, b), below, 1, depth - 1)
        inner_step(depth - 1, below, top=True)

    receive(ZB, "gz", ip.at[pl.ds(0, 4)])
    receive(ZS, "gz", s.at[0])

    for row in chunks:
        rows = slice(row, row + ROWS)
        at = slice(PAD + row, PAD + row + ROWS)
        for side, z, halo in ((0, 0, 0), (1, depth - 1, depth + 1)):
            sign = 1.0 if side else -1.0
            st = s[halo, rows, :]
            twice = 2.0 / (2.0 + s[z + 1, rows, :] + st)
            for c in range(3):
                out = mech[c, z, rows, :] + twice * (u[c, halo, at, :] - u[c, z + 1, at, :])
                if c == 2:
                    out = out + sign * (0.25 * st - 0.5 * p[halo, at, :])
                mech[c, z, rows, :] = out
            gz[z + side, rows, :] = (2.0 * sign * mask("gz", side)) * (twice * (p[halo, at, :] - p[z + 1, at, :]))
            active = base + halo - 1 < th[rows, :]
            h = 1.0 + st
            free = rows_resistance(zn[halo, rows, :], active) / (h * h * h)
            part = jnp.where(active, -h, 0.0) if side else tot[rows, :]
            tail[side, 0, rows, :] = 1.0 + scale * part
            tail[side, 1, rows, :] = free

    receive(X2, "gx", xer.at[0])
    receive(Y2, "gy", yer.at[0])

    def side_rows(z, carry):
        for side, x in ((0, 0), (1, width - 1)):
            step = (0.25 if side else -0.25) * xer[side, 0, pl.ds(z, 1), :]
            mech[0, z, x:x + 1, :] = mech[0, z, x:x + 1, :] + step
        return carry

    loop(side_rows, 0)
    mech_sides[0], mech_sides[1] = weave(
        -(0.25 * yer[0, 0] - 0.5 * yr[0, 3]), 0.25 * yer[1, 0] - 0.5 * yr[1, 3]
    )

    for off in far:
        column(off, size["gz"] - off).wait_recv()
    for off in far:
        for axis in ("gx", "gy"):
            for side in (0, 1):
                @pl.when(both(axis, 1 - side, off))
                def _():
                    edge_copy(axis, side, off, 1 - side, off).wait_recv()

    packs = (zero8, zero8)
    ends = []
    for row in chunks:
        rows = slice(row, row + ROWS)
        lower, upper = jnp.zeros((ROWS, lanes), f32), jnp.zeros((ROWS, lanes), f32)
        for off in far:
            piece = cs[off - 1, rows, :]
            below = (me["gz"] >= off).astype(f32)
            lower = lower + piece * below
            upper = upper + piece * (1.0 - below)
        off_out[rows, :] = lower
        upper = scale * upper
        packs = pack_rows(upper, 0, row, packs)
        if row == 0:
            ends.append(upper[0:1, :])
        if row + ROWS == width:
            ends.append(upper[ROWS - 1:ROWS, :])
        r[0, rows, :] = (tail[0, 0, rows, :] + upper) * tail[0, 1, rows, :]
        r[depth + 1, rows, :] = (tail[1, 0, rows, :] + upper) * tail[1, 1, rows, :]

        def burden_step(z, carry):
            r[z + 1, rows, :] = r[z + 1, rows, :] + upper * inv[z, rows, :]
            return carry

        loop(burden_step, 0)

    packed = spread(packs)
    lanes_out = []
    for side in (0, 1):
        beyond = jnp.zeros((8, lanes), f32)
        beyond_row = jnp.zeros((1, lanes), f32)
        for off in far:
            beyond = beyond + tyr[side, off - 1]
            beyond_row = beyond_row + txr[side, off - 1]
        here = (ye[side, 1] + packed[side]) * ye[side, 2]
        there = (yer[side, 1] + scale * beyond) * yer[side, 2]
        lanes_out.append((2.0 * mask("gy", side)) * (yr[side, 3] - ys[side, 3]) / (here + there))
        here = (xe[side, 1] + ends[side]) * xe[side, 2]
        there = (xer[side, 1] + scale * beyond_row) * xer[side, 2]
        sign = 1.0 if side else -1.0
        row_sides[side] = (2.0 * sign * mask("gx", side)) * (xr[side, 3] - xs[side, 3]) / (here + there)
    flow_sides[0], flow_sides[1] = weave(*lanes_out)

    for side in (0, 1):
        for i, whole in enumerate((inv.at[pl.ds(0, 7), pl.ds(0, depth)], inv.at[pl.ds(0, 7), pl.ds(0, 8)], inv.at[pl.ds(0, 6)])):
            @pl.when(has(AXES[i], side))
            def _():
                pltpu.make_async_copy(whole, whole, side_send.at[i, side]).wait()
    every = ip.at[pl.ds(0, size["gz"] - 1)]
    pltpu.make_async_copy(every, every, col_send.at[0]).wait()
    for off in far:
        for axis in ("gx", "gy"):
            for side in (0, 1):
                @pl.when(both(axis, side, -off))
                def _():
                    edge_copy(axis, side, off, side, -off).wait_send()


def finish(
    depth_total, pre, offset, r, gx, gy, gz, s, mech, flow_sides, mech_sides, row_sides,
    heights_out, flow_out, mech_out, heights, flow, mech1, fx, sem,
):
    depth, width, lanes = pre.shape
    f32 = jnp.float32
    copies = [
        pltpu.make_async_copy(mech.at[0], mech_out.at[0], sem.at[0]),
        pltpu.make_async_copy(mech.at[2], mech_out.at[2], sem.at[1]),
    ]
    for copy in copies:
        copy.start()
    lane = lax.broadcasted_iota(jnp.int32, (ROWS, lanes), 1)
    first, last = lane == 0, lane == lanes - 1
    outer = jnp.logical_or(first, last)
    chunks = range(0, width, ROWS)

    def sides(woven, z, row):
        parts = []
        for g in range(ROWS // 8):
            slot = z * (width // 8) + row // 8 + g
            parts.append(pltpu.roll(woven[(row // 8 + g) % 2], lanes - 1 - slot, 1))
        return jnp.where(outer, jnp.concatenate(parts, axis=0), 0.0)

    flow_woven, mech_woven = (flow_sides[0], flow_sides[1]), (mech_sides[0], mech_sides[1])

    def rise(z, rows):
        return gz[z, rows, :] / (r[z, rows, :] + r[z + 1, rows, :])

    def step(z, carry):
        fx[z, PAD - 1:PAD, :] = row_sides[0, pl.ds(z, 1), :]
        for row in chunks:
            rows = slice(row, row + ROWS)
            mid = r[z + 1, rows, :]
            fx[z, PAD + row:PAD + row + ROWS, :] = gx[z, rows, :] / (mid + r[z + 1, row + 1:row + 1 + ROWS, :])
        fx[z, PAD + width - 1:PAD + width, :] = row_sides[1, pl.ds(z, 1), :]
        out = []
        for row, below in zip(chunks, carry):
            rows = slice(row, row + ROWS)
            mid = r[z + 1, rows, :]
            above = rise(z + 1, rows)
            fy = gy[z, rows, :] / (mid + pltpu.roll(mid, lanes - 1, 1))
            total = (above - below) + (fy - pltpu.roll(fy, 1, 1)) - s[z + 1, rows, :]
            total = total + (fx[z, PAD + row:PAD + row + ROWS, :] - fx[z, PAD + row - 1:PAD + row - 1 + ROWS, :])
            flow[z, rows, :] = total + sides(flow_woven, z, row)
            mech1[z, rows, :] = mech[1, z, rows, :] + sides(mech_woven, z, row)
            heights[z, rows, :] = (pre[z, rows, :] + offset[rows, :]) * (1.0 / depth_total)
            out.append(above)
        return tuple(out)

    carry = tuple(rise(0, slice(row, row + ROWS)) for row in chunks)
    parts = 4 if depth % 4 == 0 else 1
    some = depth // parts
    for part in range(parts):
        carry = lax.fori_loop(part * some, (part + 1) * some, step, carry, unroll=some)
        layers = pl.ds(part * some, some)
        for i, (src, dst) in enumerate(((flow, flow_out), (heights, heights_out), (mech1, mech_out.at[1]))):
            pltpu.make_async_copy(src.at[layers], dst.at[layers], sem.at[2 + i]).start()
    for i, (src, dst) in enumerate(((flow, flow_out), (heights, heights_out), (mech1, mech_out.at[1]))):
        pltpu.make_async_copy(src, dst, sem.at[2 + i]).wait()
    for copy in copies:
        copy.wait()


def local(counts, displacement, pressure, zone, perm_table, thickness):
    _, depth, width, lanes = displacement.shape
    f32, i32 = jnp.float32, jnp.int32
    tall = (depth + 2, width + 2 * PAD, lanes)
    cells, plane = (depth, width, lanes), (width, lanes)
    hbm, vmem = (pl.BlockSpec(memory_space=m) for m in (pl.ANY, pltpu.VMEM))
    far = max(counts[2] - 1, 1)
    V = lambda *shape, dtype=f32: pltpu.VMEM(shape, dtype)
    D = pltpu.SemaphoreType.DMA
    inputs = [
        pltpu.with_memory_space_constraint(x, pltpu.HBM)
        for x in (displacement, pressure, zone, perm_table, thickness)
    ]
    results = (
        V(*cells),
        V(*plane),
        V(depth + 2, width + 8, lanes),
        V(*cells),
        V(*cells),
        V(depth + 1, width, lanes),
        V(depth + 2, width, lanes),
        V(3, *cells),
        V(2, 8, lanes),
        V(2, 8, lanes),
        V(2, depth, lanes),
    )
    fields = pl.pallas_call(
        functools.partial(kernel, counts),
        out_shape=results,
        in_specs=[hbm] * 5,
        out_specs=(vmem,) * len(results),
        scratch_shapes=[
            V(3, *tall), V(*tall), V(depth, width + 2 * PAD, lanes), V(depth + 2, width, lanes, dtype=i32),
            V(*plane, dtype=i32), pltpu.SMEM((ZONES,), f32), V(*cells), V(*cells), V(*plane), V(2, 2, *plane),
            V(2, 4, depth, lanes), V(2, 4, depth, lanes), V(2, 4, 8, lanes), V(2, 4, 8, lanes),
            V(2, 3, depth, lanes), V(2, 3, depth, lanes), V(2, 3, 8, lanes), V(2, 3, 8, lanes),
            V(2, depth, lanes, dtype=i32), V(2, 8, lanes, dtype=i32),
            V(2, 1, lanes), V(2, far, 1, lanes), V(2, 8, lanes), V(2, far, 8, lanes), V(far, *plane),
            D((7,)), D((9, 2)), D((3, 2)), D((1,)), D((far,)), D((2, 2, far)), D((2, 2, far)),
        ],
        compiler_params=pltpu.CompilerParams(
            collective_id=0, has_side_effects=True, vmem_limit_bytes=40 * 2**20
        ),
    )(*inputs)
    return pl.pallas_call(
        functools.partial(finish, depth * counts[2]),
        out_shape=tuple(jax.ShapeDtypeStruct(x.shape, f32) for x in (pressure, pressure, displacement)),
        in_specs=[vmem] * len(results),
        out_specs=(hbm,) * 3,
        scratch_shapes=[V(*cells), V(*cells), V(*cells), V(depth, width + 2 * PAD, lanes), D((5,))],
        compiler_params=pltpu.CompilerParams(vmem_limit_bytes=8 * 2**20),
    )(*[pltpu.with_memory_space_constraint(x, pltpu.VMEM) for x in fields])


def solution(mesh):
    counts = tuple(mesh.shape[axis] for axis in AXES)
    in_specs = (
        P(None, "gz", "gx", "gy"),
        P("gz", "gx", "gy"),
        P("gz", "gx", "gy"),
        P(),
        P("gx", "gy"),
    )
    out_specs = (P("gz", "gx", "gy"), P("gz", "gx", "gy"), P(None, "gz", "gx", "gy"))
    return jax.shard_map(
        functools.partial(local, counts), mesh=mesh, in_specs=in_specs, out_specs=out_specs, check_vma=False
    )
```

```python
import functools

import jax
import jax.numpy as jnp
from jax import lax
from jax.experimental import pallas as pl
from jax.experimental.pallas import tpu as pltpu
from jax.sharding import PartitionSpec as P

MESH = pl.DeviceIdType.MESH
ZONES = 8
AXES = ("gx", "gy", "gz")
PAD = 8
ROWS = 32

ZU, ZB, X0, Y0, X1, Y1, ZS, X2, Y2 = range(9)


def kernel(
    counts, disp, press, zone, table, thick,
    pre, off_out, r, gx, gy, gz, s, mech, flow_sides, mech_sides, row_sides,
    u, p, t, zn, th, tab, ip, inv, tot, tail,
    xs, xr, ys, yr, xe, xer, ye, yer, zr, zp, tx, txr, ty, tyr, cs,
    load_sem, recv_sem, side_send, col_send, col_recv, edge_send, edge_recv,
):
    depth, width, lanes = press.shape
    groups = width // 8
    last = PAD + width
    me = {axis: lax.axis_index(axis) for axis in AXES}
    size = dict(zip(AXES, counts))
    depth_total = depth * size["gz"]
    scale = 2.0 / depth_total
    own = pl.ds(PAD, width)
    f32 = jnp.float32
    chunks = range(0, width, ROWS)
    far = range(1, size["gz"])

    def has(axis, side):
        return me[axis] > 0 if side == 0 else me[axis] < size[axis] - 1

    def mask(axis, side):
        return has(axis, side).astype(f32)

    def peer(axis, side, up=0):
        place = {axis: me[axis] + (1 if side else -1)}
        if up:
            place["gz"] = me["gz"] + up
        return place

    def round_z(off):
        return {"gz": lax.rem(me["gz"] + off, size["gz"])}

    def both(axis, side, off):
        inside = me["gz"] + off < size["gz"] if off > 0 else me["gz"] + off >= 0
        return jnp.logical_and(has(axis, side), inside)

    def loop(step, carry, start=0, end=depth):
        return lax.fori_loop(start, end, step, carry, unroll=end - start)

    inner = pl.ds(1, depth)
    loads = [
        pltpu.make_async_copy(disp.at[1], u.at[1, inner, own], load_sem.at[0]),
        pltpu.make_async_copy(disp.at[0], u.at[0, inner, own], load_sem.at[1]),
        pltpu.make_async_copy(disp.at[2], u.at[2, inner, own], load_sem.at[2]),
        pltpu.make_async_copy(press, p.at[inner, own], load_sem.at[3]),
        pltpu.make_async_copy(zone, zn.at[inner], load_sem.at[4]),
        pltpu.make_async_copy(thick, th, load_sem.at[5]),
        pltpu.make_async_copy(table, tab, load_sem.at[6]),
    ]
    for load in loads:
        load.start()

    barrier = pltpu.get_barrier_semaphore()
    partners = jnp.int32(size["gz"] - 1)
    for axis in ("gx", "gy"):
        for side in (0, 1):
            @pl.when(has(axis, side))
            def _():
                pl.semaphore_signal(barrier, inc=1, device_id=peer(axis, side), device_id_type=MESH)
            for off in far:
                @pl.when(both(axis, side, off))
                def _():
                    pl.semaphore_signal(barrier, inc=1, device_id=peer(axis, side, off), device_id_type=MESH)
            partners = partners + has(axis, side).astype(jnp.int32) * (1 + me["gz"])
    for off in far:
        pl.semaphore_signal(barrier, inc=1, device_id=round_z(off), device_id_type=MESH)

    def copy(message, axis, side, src, dst, at):
        return pltpu.make_async_remote_copy(
            src_ref=src,
            dst_ref=dst,
            send_sem=side_send.at[AXES.index(axis), side],
            recv_sem=recv_sem.at[message, side],
            device_id=peer(axis, at),
            device_id_type=MESH,
        )

    def send(message, axis, *parts):
        for side in (0, 1):
            @pl.when(has(axis, side))
            def _():
                for srcs, dsts in parts:
                    copy(message, axis, side, srcs[side], dsts[1 - side], side).start()

    def receive(message, axis, whole):
        for side in (0, 1):
            @pl.when(has(axis, side))
            def _():
                pltpu.make_async_copy(whole, whole, recv_sem.at[message, 1 - side]).wait()

    def clear(axis, refs):
        for side in (0, 1):
            @pl.when(jnp.logical_not(has(axis, side)))
            def _():
                for ref in refs[side]:
                    ref[...] = jnp.zeros(ref.shape, ref.dtype)

    def pair(ref, *at):
        return (ref.at[(0, *at)], ref.at[(1, *at)])

    zu = ((disp.at[2, 0], disp.at[2, depth - 1]), (u.at[2, 0, own], u.at[2, depth + 1, own]))
    zl = (
        (disp.at[pl.ds(0, 2), 0], disp.at[pl.ds(0, 2), depth - 1]),
        (u.at[pl.ds(0, 2), 0, own], u.at[pl.ds(0, 2), depth + 1, own]),
    )
    zq = ((press.at[0], press.at[depth - 1]), (p.at[0, own], p.at[depth + 1, own]))
    zz = ((zone.at[0], zone.at[depth - 1]), (zn.at[0], zn.at[depth + 1]))
    zs = ((s.at[1], s.at[depth]), (s.at[0], s.at[depth + 1]))
    x0, y0 = (pair(xs, 0), pair(xr, 0)), (pair(ys, 0), pair(yr, 0))
    x1, y1 = (pair(xs, pl.ds(1, 3)), pair(xr, pl.ds(1, 3))), (pair(ys, pl.ds(1, 3)), pair(yr, pl.ds(1, 3)))
    x2, y2 = (pair(xe), pair(xer)), (pair(ye), pair(yer))

    lane = lax.broadcasted_iota(jnp.int32, (8, lanes), 1)
    odd = lax.rem(lane, 2) == 1
    lane_r = lax.broadcasted_iota(jnp.int32, (ROWS, lanes), 1)
    first_lane, last_lane = lane_r == 0, lane_r == lanes - 1
    zero8 = jnp.zeros((8, lanes), f32)

    def pack(values, slot, packs):
        turned = pltpu.roll(values, slot, 1)
        low = jnp.where(lane == slot, turned, packs[0])
        return low, jnp.where(lane == lax.rem(slot + lanes - 1, lanes), turned, packs[1])

    def keep(ref, packs, *at):
        ref[(0, *at)] = packs[0]
        ref[(1, *at)] = pltpu.roll(packs[1], 1, 1)

    def pack_rows(values, z, row, packs):
        for g in range(values.shape[0] // 8):
            packs = pack(values[8 * g:8 * g + 8, :], z * groups + row // 8 + g, packs)
        return packs

    def weave(low, high):
        low = pltpu.roll(low, 1, 1)
        return jnp.where(odd, low, high), jnp.where(odd, high, low)

    def ends_at(woven, z, row):
        parts = []
        for g in range(ROWS // 8):
            slot = z * groups + row // 8 + g
            parts.append(pltpu.roll(woven[(row // 8 + g) % 2], lanes - 1 - slot, 1))
        return jnp.concatenate(parts, axis=0)

    def yshift(v, ends):
        below, above = pltpu.roll(v, 1, 1), pltpu.roll(v, lanes - 1, 1)
        return jnp.where(first_lane, ends, below), jnp.where(last_lane, ends, above)

    fields = [u.at[0], u.at[1], u.at[2], p]

    def pack_field(i, n):
        def step(z, packs):
            return pack_rows(fields[i][z + 1, PAD:last, :], z, 0, packs)

        keep(ys, loop(step, (zero8, zero8)), n)

    def take_rows(i):
        def step(z, carry):
            xs[0, i, pl.ds(z, 1), :] = fields[i][z + 1, PAD:PAD + 1, :]
            xs[1, i, pl.ds(z, 1), :] = fields[i][z + 1, last - 1:last, :]
            return carry

        loop(step, 0)

    loads[0].wait()
    pack_field(1, 0)
    loads[1].wait()
    take_rows(0)
    pl.semaphore_wait(barrier, partners)
    send(ZU, "gz", zu)
    send(X0, "gx", x0)
    send(Y0, "gy", y0)
    send(ZB, "gz", zl, zq, zz)

    loads[2].wait()
    loads[3].wait()
    for i in range(1, 4):
        take_rows(i)
    pack_field(0, 1)
    pack_field(2, 2)
    pack_field(3, 3)
    send(X1, "gx", x1)
    send(Y1, "gy", y1)

    clear("gx", [[ref.at[side] for ref in (xr, xer)] for side in (0, 1)])
    clear("gy", [[ref.at[side] for ref in (yr, yer)] for side in (0, 1)])
    edges = (0, depth + 1)
    clear("gz", [[u.at[:, z, own], p.at[z, own], s.at[z], zn.at[z]] for z in edges])
    for axis, ref in (("gx", txr), ("gy", tyr)):
        for side in (0, 1):
            for off in far:
                @pl.when(jnp.logical_not(both(axis, side, off)))
                def _():
                    ref[side, off - 1] = jnp.zeros(ref.shape[2:], f32)

    for load in loads[4:]:
        load.wait()
    base = me["gz"] * depth

    inverse = [1.0 / jnp.full((8, lanes), tab[i], f32) for i in range(ZONES)]

    def rows_resistance(zones, active):
        count = zones.shape[0] // 8
        least = jnp.concatenate([inverse[0]] * count, axis=0)
        for i in range(1, ZONES):
            least = jnp.where(zones == i, jnp.concatenate([inverse[i]] * count, axis=0), least)
        return jnp.where(active, least * (1.0 / (0.001 + 0.999)), least * (1.0 / 0.001))

    def zone_step(z, packs):
        for row in chunks:
            zones = zn[z + 1, row:row + ROWS, :]
            ip[z, row:row + ROWS, :] = rows_resistance(zones, base + z < th[row:row + ROWS, :])
            packs = pack_rows(zones, z, row, packs)
        zr[0, pl.ds(z, 1), :] = zn[z + 1, 0:1, :]
        zr[1, pl.ds(z, 1), :] = zn[z + 1, width - 1:width, :]
        return packs

    none8 = jnp.zeros((8, lanes), jnp.int32)
    keep(zp, loop(zone_step, (none8, none8)))

    def spread(packs):
        step = groups
        while step < lanes:
            turned = [pltpu.roll(x, step, 1) for x in packs]
            packs = [x + y for x, y in zip(packs, turned)]
            step *= 2
        return packs

    edge_height = pack_rows(th[...], 0, 0, (none8, none8))
    edge_height = spread([edge_height[0], pltpu.roll(edge_height[1], 1, 1)])
    edge_layer = base + lane // groups

    receive(ZU, "gz", zu[1][0])
    receive(X0, "gx", xr.at[0, 0])
    receive(Y0, "gy", yr.at[0, 0])

    def unpack_first(z, carry):
        u[0, z + 1, PAD - 1:PAD, :] = xr[0, 0, pl.ds(z, 1), :]
        u[0, z + 1, last:last + 1, :] = xr[1, 0, pl.ds(z, 1), :]
        return carry

    loop(unpack_first, 0)

    woven = weave(yr[0, 0], yr[1, 0])
    for row in chunks:
        rows = slice(row, row + ROWS)
        at = slice(PAD + row, PAD + row + ROWS)
        height = th[rows, :]

        def strain_step(z, acc):
            up = u[0, z + 1, PAD + row + 1:PAD + row + 1 + ROWS, :]
            down = u[0, z + 1, PAD + row - 1:PAD + row - 1 + ROWS, :]
            ym, yp = yshift(u[1, z + 1, at, :], ends_at(woven, z, row))
            div = 0.5 * ((up - down) + (yp - ym) + (u[2, z + 2, at, :] - u[2, z, at, :]))
            st = 0.3 * jnp.tanh(div)
            s[z + 1, rows, :] = st
            t[z, at, :] = 0.25 * st - 0.5 * p[z + 1, at, :]
            if row == 0:
                xe[0, 0, pl.ds(z, 1), :] = st[0:1, :]
            if row + ROWS == width:
                xe[1, 0, pl.ds(z, 1), :] = st[ROWS - 1:ROWS, :]
            acc = acc + jnp.where(base + z < height, 1.0 + st, 0.0)
            pre[z, rows, :] = acc
            return acc

        tot[rows, :] = loop(strain_step, jnp.zeros((ROWS, lanes), f32))

    def column(off, at):
        return pltpu.make_async_remote_copy(
            src_ref=tot,
            dst_ref=cs.at[off - 1],
            send_sem=col_send.at[0],
            recv_sem=col_recv.at[off - 1],
            device_id=round_z(at),
            device_id_type=MESH,
        )

    for side, row in ((0, 0), (1, width - 1)):
        tx[side] = tot[row:row + 1, :]
    keep(ty, pack_rows(tot[...], 0, 0, (zero8, zero8)))

    def edge_copy(axis, side, off, at, up):
        i = ("gx", "gy").index(axis)
        src, dst = ((tx, txr), (ty, tyr))[i]
        return pltpu.make_async_remote_copy(
            src_ref=src.at[side],
            dst_ref=dst.at[1 - side, off - 1],
            send_sem=edge_send.at[i, side, off - 1],
            recv_sem=edge_recv.at[i, side, off - 1],
            device_id=peer(axis, at, up),
            device_id_type=MESH,
        )

    for off in far:
        for axis in ("gx", "gy"):
            for side in (0, 1):
                @pl.when(both(axis, side, -off))
                def _():
                    edge_copy(axis, side, off, side, -off).start()
    for off in far:
        column(off, off).start()
    send(ZS, "gz", zs)

    packs = loop(lambda z, packs: pack_rows(s[z + 1], z, 0, packs), (zero8, zero8))
    edge = packs[0], pltpu.roll(packs[1], 1, 1)
    actives = [edge_layer < edge_height[side] for side in (0, 1)]
    thicknesses = [jnp.where(actives[side], 1.0 + edge[side], 0.0) for side in (0, 1)]
    aboves, step = thicknesses, groups
    while step < lanes:
        turned = [pltpu.roll(x, lanes - step, 1) for x in aboves]
        aboves = [x + jnp.where(lane < lanes - step, y, 0.0) for x, y in zip(aboves, turned)]
        step *= 2
    for side in (0, 1):
        st, active, thickness = edge[side], actives[side], thicknesses[side]
        h = 1.0 + st
        ye[side, 0] = st
        ye[side, 1] = 1.0 + scale * (aboves[side] - thickness)
        ye[side, 2] = rows_resistance(zp[side], active) / (h * h * h)
        row = (width - 1) * side

        def row_step(z, carry):
            xe[side, 1, pl.ds(z, 1), :] = 1.0 + scale * (tot[row:row + 1, :] - pre[z, row:row + 1, :])
            return carry

        loop(row_step, 0)
        h = 1.0 + xe[side, 0]
        layer = base + lax.broadcasted_iota(jnp.int32, (depth, lanes), 0)
        xe[side, 2] = rows_resistance(zr[side], layer < th[row:row + 1, :]) / (h * h * h)

    send(X2, "gx", x2)
    send(Y2, "gy", y2)

    receive(X1, "gx", xr.at[0, pl.ds(1, 3)])
    receive(Y1, "gy", yr.at[0, pl.ds(1, 3)])

    def unpack_inputs(z, carry):
        for side, at in ((0, PAD - 1), (1, last)):
            for i in (1, 2):
                fields[i][z + 1, at:at + 1, :] = xr[side, i, pl.ds(z, 1), :]
            t[z, at:at + 1, :] = -0.5 * xr[side, 3, pl.ds(z, 1), :]
        return carry

    loop(unpack_inputs, 0)

    wovens = [weave(yr[0, n], yr[1, n]) for n in (1, 0, 2)]
    for row in chunks:
        rows = slice(row, row + ROWS)
        at = slice(PAD + row, PAD + row + ROWS)
        up1 = slice(PAD + row + 1, PAD + row + 1 + ROWS)
        down1 = slice(PAD + row - 1, PAD + row - 1 + ROWS)
        height = tot[rows, :]

        def inner_step(z, below, bottom=False, top=False):
            mids = [u[c, z + 1, at, :] for c in range(3)]
            pm, st, tm = p[z + 1, at, :], s[z + 1, rows, :], t[z, at, :]
            above = None
            if not top:
                twice = 2.0 / (2.0 + st + s[z + 2, rows, :])
                above = [twice * (u[c, z + 2, at, :] - mids[c]) for c in range(3)]
                gz[z + 1, rows, :] = 2.0 * twice * (p[z + 2, at, :] - pm)
            tb, ta = pltpu.roll(tm, 1, 1), pltpu.roll(tm, lanes - 1, 1)
            grads = [
                t[z, up1, :] - t[z, down1, :],
                jnp.where(last_lane, 0.0, ta) - jnp.where(first_lane, 0.0, tb),
            ]
            if bottom:
                grads.append(t[z + 1, at, :])
            elif top:
                grads.append(-t[z - 1, at, :])
            else:
                grads.append(t[z + 1, at, :] - t[z - 1, at, :])
            for c in range(3):
                ym, yp = yshift(mids[c], ends_at(wovens[c], z, row))
                out = u[c, z + 1, up1, :] + u[c, z + 1, down1, :] + ym + yp - 4.0 * mids[c] + grads[c]
                if not top:
                    out = out + above[c]
                if not bottom:
                    out = out - below[c]
                mech[c, z, rows, :] = out
            gx[z, rows, :] = 2.0 * (p[z + 1, up1, :] - pm)
            gy[z, rows, :] = jnp.where(last_lane, 0.0, 2.0 * (pltpu.roll(pm, lanes - 1, 1) - pm))
            h = 1.0 + st
            free = ip[z, rows, :] / (h * h * h)
            inv[z, rows, :] = free
            r[z + 1, rows, :] = free + (scale * (height - pre[z, rows, :])) * free
            return tuple(above) if above else None

        below = inner_step(0, None, bottom=True)
        below = loop(lambda z, b: inner_step(z, b), below, 1, depth - 1)
        inner_step(depth - 1, below, top=True)

    receive(ZB, "gz", ip.at[pl.ds(0, 4)])
    receive(ZS, "gz", s.at[0])

    for row in chunks:
        rows = slice(row, row + ROWS)
        at = slice(PAD + row, PAD + row + ROWS)
        for side, z, halo in ((0, 0, 0), (1, depth - 1, depth + 1)):
            sign = 1.0 if side else -1.0
            st = s[halo, rows, :]
            twice = 2.0 / (2.0 + s[z + 1, rows, :] + st)
            for c in range(3):
                out = mech[c, z, rows, :] + twice * (u[c, halo, at, :] - u[c, z + 1, at, :])
                if c == 2:
                    out = out + sign * (0.25 * st - 0.5 * p[halo, at, :])
                mech[c, z, rows, :] = out
            gz[z + side, rows, :] = (2.0 * sign * mask("gz", side)) * (twice * (p[halo, at, :] - p[z + 1, at, :]))
            active = base + halo - 1 < th[rows, :]
            h = 1.0 + st
            free = rows_resistance(zn[halo, rows, :], active) / (h * h * h)
            part = jnp.where(active, -h, 0.0) if side else tot[rows, :]
            tail[side, 0, rows, :] = 1.0 + scale * part
            tail[side, 1, rows, :] = free

    receive(X2, "gx", xer.at[0])
    receive(Y2, "gy", yer.at[0])

    def side_rows(z, carry):
        for side, x in ((0, 0), (1, width - 1)):
            step = (0.25 if side else -0.25) * xer[side, 0, pl.ds(z, 1), :]
            mech[0, z, x:x + 1, :] = mech[0, z, x:x + 1, :] + step
        return carry

    loop(side_rows, 0)
    mech_sides[0], mech_sides[1] = weave(
        -(0.25 * yer[0, 0] - 0.5 * yr[0, 3]), 0.25 * yer[1, 0] - 0.5 * yr[1, 3]
    )

    for off in far:
        column(off, size["gz"] - off).wait_recv()
    for off in far:
        for axis in ("gx", "gy"):
            for side in (0, 1):
                @pl.when(both(axis, 1 - side, off))
                def _():
                    edge_copy(axis, side, off, 1 - side, off).wait_recv()

    packs = (zero8, zero8)
    ends = []
    for row in chunks:
        rows = slice(row, row + ROWS)
        lower, upper = jnp.zeros((ROWS, lanes), f32), jnp.zeros((ROWS, lanes), f32)
        for off in far:
            piece = cs[off - 1, rows, :]
            below = (me["gz"] >= off).astype(f32)
            lower = lower + piece * below
            upper = upper + piece * (1.0 - below)
        off_out[rows, :] = lower
        upper = scale * upper
        packs = pack_rows(upper, 0, row, packs)
        if row == 0:
            ends.append(upper[0:1, :])
        if row + ROWS == width:
            ends.append(upper[ROWS - 1:ROWS, :])
        r[0, rows, :] = (tail[0, 0, rows, :] + upper) * tail[0, 1, rows, :]
        r[depth + 1, rows, :] = (tail[1, 0, rows, :] + upper) * tail[1, 1, rows, :]

        def burden_step(z, carry):
            r[z + 1, rows, :] = r[z + 1, rows, :] + upper * inv[z, rows, :]
            return carry

        loop(burden_step, 0)

    beyonds = [functools.reduce(lambda x, y: x + y, [tyr[side, off - 1] for off in far], zero8) for side in (0, 1)]
    packed = spread([packs[0], pltpu.roll(packs[1], 1, 1), *(scale * x for x in beyonds)])
    lanes_out = []
    for side in (0, 1):
        beyond_row = jnp.zeros((1, lanes), f32)
        for off in far:
            beyond_row = beyond_row + txr[side, off - 1]
        here = (ye[side, 1] + packed[side]) * ye[side, 2]
        there = (yer[side, 1] + packed[2 + side]) * yer[side, 2]
        lanes_out.append((2.0 * mask("gy", side)) * (yr[side, 3] - ys[side, 3]) / (here + there))
        here = (xe[side, 1] + ends[side]) * xe[side, 2]
        there = (xer[side, 1] + scale * beyond_row) * xer[side, 2]
        sign = 1.0 if side else -1.0
        row_sides[side] = (2.0 * sign * mask("gx", side)) * (xr[side, 3] - xs[side, 3]) / (here + there)
    flow_sides[0], flow_sides[1] = weave(*lanes_out)

    for side in (0, 1):
        for i, whole in enumerate((inv.at[pl.ds(0, 7), pl.ds(0, depth)], inv.at[pl.ds(0, 7), pl.ds(0, 8)], inv.at[pl.ds(0, 6)])):
            @pl.when(has(AXES[i], side))
            def _():
                pltpu.make_async_copy(whole, whole, side_send.at[i, side]).wait()
    every = ip.at[pl.ds(0, size["gz"] - 1)]
    pltpu.make_async_copy(every, every, col_send.at[0]).wait()
    for off in far:
        for axis in ("gx", "gy"):
            for side in (0, 1):
                @pl.when(both(axis, side, -off))
                def _():
                    edge_copy(axis, side, off, side, -off).wait_send()


def finish(
    depth_total, pre, offset, r, gx, gy, gz, s, mech, flow_sides, mech_sides, row_sides,
    heights_out, flow_out, mech_out, heights, flow, mech1, fx, fy, sem,
):
    depth, width, lanes = pre.shape
    f32 = jnp.float32
    copies = [
        pltpu.make_async_copy(mech.at[0], mech_out.at[0], sem.at[0]),
        pltpu.make_async_copy(mech.at[2], mech_out.at[2], sem.at[1]),
    ]
    for copy in copies:
        copy.start()
    lane = lax.broadcasted_iota(jnp.int32, (ROWS, lanes), 1)
    first, last = lane == 0, lane == lanes - 1
    outer = jnp.logical_or(first, last)
    chunks = range(0, width, ROWS)

    def sides(woven, z, row):
        parts = []
        for g in range(ROWS // 8):
            slot = z * (width // 8) + row // 8 + g
            parts.append(pltpu.roll(woven[(row // 8 + g) % 2], lanes - 1 - slot, 1))
        return jnp.where(outer, jnp.concatenate(parts, axis=0), 0.0)

    flow_woven, mech_woven = (flow_sides[0], flow_sides[1]), (mech_sides[0], mech_sides[1])

    def rise(z, rows):
        return gz[z, rows, :] / (r[z, rows, :] + r[z + 1, rows, :])

    def lateral(z, carry):
        fx[z, PAD - 1:PAD, :] = row_sides[0, pl.ds(z, 1), :]
        mid = r[z + 1, 0:width, :]
        fy[z] = gy[z] / (mid + pltpu.roll(mid, lanes - 1, 1))
        fx[z, PAD:PAD + width, :] = gx[z] / (mid + r[z + 1, 1:width + 1, :])
        fx[z, PAD + width - 1:PAD + width, :] = row_sides[1, pl.ds(z, 1), :]
        return carry

    def step(z, carry):
        out = []
        for row, below in zip(chunks, carry):
            rows = slice(row, row + ROWS)
            above = rise(z + 1, rows)
            face = fy[z, rows, :]
            total = (above - below) + (face - pltpu.roll(face, 1, 1)) - s[z + 1, rows, :]
            total = total + (fx[z, PAD + row:PAD + row + ROWS, :] - fx[z, PAD + row - 1:PAD + row - 1 + ROWS, :])
            flow[z, rows, :] = total + sides(flow_woven, z, row)
            mech1[z, rows, :] = mech[1, z, rows, :] + sides(mech_woven, z, row)
            heights[z, rows, :] = (pre[z, rows, :] + offset[rows, :]) * (1.0 / depth_total)
            out.append(above)
        return tuple(out)

    carry = tuple(rise(0, slice(row, row + ROWS)) for row in chunks)
    parts = 4 if depth % 4 == 0 else 1
    some = depth // parts
    for part in range(parts):
        span = part * some, (part + 1) * some
        lax.fori_loop(*span, lateral, 0, unroll=some)
        carry = lax.fori_loop(*span, step, carry, unroll=some)
        layers = pl.ds(part * some, some)
        for i, (src, dst) in enumerate(((flow, flow_out), (heights, heights_out), (mech1, mech_out.at[1]))):
            pltpu.make_async_copy(src.at[layers], dst.at[layers], sem.at[2 + i]).start()
    for i, (src, dst) in enumerate(((flow, flow_out), (heights, heights_out), (mech1, mech_out.at[1]))):
        pltpu.make_async_copy(src, dst, sem.at[2 + i]).wait()
    for copy in copies:
        copy.wait()


def local(counts, displacement, pressure, zone, perm_table, thickness):
    _, depth, width, lanes = displacement.shape
    f32, i32 = jnp.float32, jnp.int32
    tall = (depth + 2, width + 2 * PAD, lanes)
    cells, plane = (depth, width, lanes), (width, lanes)
    hbm, vmem = (pl.BlockSpec(memory_space=m) for m in (pl.ANY, pltpu.VMEM))
    far = max(counts[2] - 1, 1)
    V = lambda *shape, dtype=f32: pltpu.VMEM(shape, dtype)
    D = pltpu.SemaphoreType.DMA
    inputs = [
        pltpu.with_memory_space_constraint(x, pltpu.HBM)
        for x in (displacement, pressure, zone, perm_table, thickness)
    ]
    results = (
        V(*cells),
        V(*plane),
        V(depth + 2, width + 8, lanes),
        V(*cells),
        V(*cells),
        V(depth + 1, width, lanes),
        V(depth + 2, width, lanes),
        V(3, *cells),
        V(2, 8, lanes),
        V(2, 8, lanes),
        V(2, depth, lanes),
    )
    fields = pl.pallas_call(
        functools.partial(kernel, counts),
        out_shape=results,
        in_specs=[hbm] * 5,
        out_specs=(vmem,) * len(results),
        scratch_shapes=[
            V(3, *tall), V(*tall), V(depth, width + 2 * PAD, lanes), V(depth + 2, width, lanes, dtype=i32),
            V(*plane, dtype=i32), pltpu.SMEM((ZONES,), f32), V(*cells), V(*cells), V(*plane), V(2, 2, *plane),
            V(2, 4, depth, lanes), V(2, 4, depth, lanes), V(2, 4, 8, lanes), V(2, 4, 8, lanes),
            V(2, 3, depth, lanes), V(2, 3, depth, lanes), V(2, 3, 8, lanes), V(2, 3, 8, lanes),
            V(2, depth, lanes, dtype=i32), V(2, 8, lanes, dtype=i32),
            V(2, 1, lanes), V(2, far, 1, lanes), V(2, 8, lanes), V(2, far, 8, lanes), V(far, *plane),
            D((7,)), D((9, 2)), D((3, 2)), D((1,)), D((far,)), D((2, 2, far)), D((2, 2, far)),
        ],
        compiler_params=pltpu.CompilerParams(
            collective_id=0, has_side_effects=True, vmem_limit_bytes=40 * 2**20
        ),
    )(*inputs)
    return pl.pallas_call(
        functools.partial(finish, depth * counts[2]),
        out_shape=tuple(jax.ShapeDtypeStruct(x.shape, f32) for x in (pressure, pressure, displacement)),
        in_specs=[vmem] * len(results),
        out_specs=(hbm,) * 3,
        scratch_shapes=[V(*cells), V(*cells), V(*cells), V(depth, width + 2 * PAD, lanes), V(*cells), D((5,))],
        compiler_params=pltpu.CompilerParams(vmem_limit_bytes=8 * 2**20),
    )(*[pltpu.with_memory_space_constraint(x, pltpu.VMEM) for x in fields])


def solution(mesh):
    counts = tuple(mesh.shape[axis] for axis in AXES)
    in_specs = (
        P(None, "gz", "gx", "gy"),
        P("gz", "gx", "gy"),
        P("gz", "gx", "gy"),
        P(),
        P("gx", "gy"),
    )
    out_specs = (P("gz", "gx", "gy"), P("gz", "gx", "gy"), P(None, "gz", "gx", "gy"))
    return jax.shard_map(
        functools.partial(local, counts), mesh=mesh, in_specs=in_specs, out_specs=out_specs, check_vma=False
    )
```

```python
import functools

import jax
import jax.numpy as jnp
from jax import lax
from jax.experimental import pallas as pl
from jax.experimental.pallas import tpu as pltpu
from jax.sharding import PartitionSpec as P

MESH = pl.DeviceIdType.MESH
ZONES = 8
AXES = ("gx", "gy", "gz")
PAD = 8
ROWS = 32

ZU, ZB, X0, Y0, X1, Y1, ZS, X2, Y2 = range(9)


def kernel(
    counts, disp, press, zone, table, thick,
    pre, cs, r, inv, gx, gy, gz, s, mech, gxe, gye, xe, xer, ye, yer, txr, tyr,
    u, p, t, zn, th, tab, ip, tot, xs, xr, ys, yr, zr, zp, tx, ty, tall_x, tall_y,
    load_sem, recv_sem, side_send, col_send, col_recv, edge_send, edge_recv,
):
    depth, width, lanes = press.shape
    groups = width // 8
    last = PAD + width
    me = {axis: lax.axis_index(axis) for axis in AXES}
    size = dict(zip(AXES, counts))
    depth_total = depth * size["gz"]
    scale = 2.0 / depth_total
    own = pl.ds(PAD, width)
    f32 = jnp.float32
    chunks = range(0, width, ROWS)
    far = range(1, size["gz"])

    def has(axis, side):
        return me[axis] > 0 if side == 0 else me[axis] < size[axis] - 1

    def mask(axis, side):
        return has(axis, side).astype(f32)

    def peer(axis, side, up=None):
        place = {axis: me[axis] + (1 if side else -1)}
        if up is not None:
            place["gz"] = me["gz"] + up
        return place

    def round_z(off):
        return {"gz": lax.rem(me["gz"] + off, size["gz"])}

    def both(axis, side, off):
        inside = me["gz"] + off < size["gz"] if off > 0 else me["gz"] + off >= 0
        return jnp.logical_and(has(axis, side), inside)

    def loop(step, carry, start=0, end=depth):
        return lax.fori_loop(start, end, step, carry, unroll=end - start)

    inner = pl.ds(1, depth)
    loads = [
        pltpu.make_async_copy(disp.at[1], u.at[1, inner, own], load_sem.at[0]),
        pltpu.make_async_copy(disp.at[0], u.at[0, inner, own], load_sem.at[1]),
        pltpu.make_async_copy(disp.at[2], u.at[2, inner, own], load_sem.at[2]),
        pltpu.make_async_copy(press, p.at[inner, own], load_sem.at[3]),
        pltpu.make_async_copy(zone, zn.at[inner], load_sem.at[4]),
        pltpu.make_async_copy(thick, th, load_sem.at[5]),
        pltpu.make_async_copy(table, tab, load_sem.at[6]),
    ]
    loads[0].start()

    barrier = pltpu.get_barrier_semaphore()
    partners = jnp.int32(size["gz"] - 1)
    for axis in ("gx", "gy"):
        for side in (0, 1):
            @pl.when(has(axis, side))
            def _():
                pl.semaphore_signal(barrier, inc=1, device_id=peer(axis, side), device_id_type=MESH)
            partners = partners + has(axis, side).astype(jnp.int32) * (1 + me["gz"])
    for off in far:
        pl.semaphore_signal(barrier, inc=1, device_id=round_z(off), device_id_type=MESH)
    for load in loads[1:]:
        load.start()
    for axis in ("gx", "gy"):
        for side in (0, 1):
            for off in far:
                @pl.when(both(axis, side, off))
                def _():
                    pl.semaphore_signal(barrier, inc=1, device_id=peer(axis, side, off), device_id_type=MESH)

    def copy(message, axis, side, src, dst, at):
        return pltpu.make_async_remote_copy(
            src_ref=src,
            dst_ref=dst,
            send_sem=side_send.at[AXES.index(axis)],
            recv_sem=recv_sem.at[message],
            device_id=peer(axis, at),
            device_id_type=MESH,
        )

    def send(message, axis, *parts):
        for side in (0, 1):
            @pl.when(has(axis, side))
            def _():
                for srcs, dsts in parts:
                    copy(message, axis, side, srcs[side], dsts[1 - side], side).start()

    def sides_of(axis):
        return has(axis, 0).astype(jnp.int32) + has(axis, 1).astype(jnp.int32)

    def finished(sem, axis, part):
        for n in (1, 2):
            @pl.when(sides_of(axis) == n)
            def _():
                pltpu.make_async_copy(part(n), part(n), sem).wait()

    def receive(message, axis, part):
        finished(recv_sem.at[message], axis, part)

    def clear(axis, refs):
        for side in (0, 1):
            @pl.when(jnp.logical_not(has(axis, side)))
            def _():
                for ref in refs[side]:
                    ref[...] = jnp.zeros(ref.shape, ref.dtype)

    def pair(ref, *at):
        return (ref.at[(0, *at)], ref.at[(1, *at)])

    zu = ((disp.at[2, 0], disp.at[2, depth - 1]), (u.at[2, 0, own], u.at[2, depth + 1, own]))
    zl = (
        (disp.at[pl.ds(0, 2), 0], disp.at[pl.ds(0, 2), depth - 1]),
        (u.at[pl.ds(0, 2), 0, own], u.at[pl.ds(0, 2), depth + 1, own]),
    )
    zq = ((press.at[0], press.at[depth - 1]), (p.at[0, own], p.at[depth + 1, own]))
    zz = ((zone.at[0], zone.at[depth - 1]), (zn.at[0], zn.at[depth + 1]))
    zs = ((s.at[1], s.at[depth]), (s.at[0], s.at[depth + 1]))
    x0, y0 = (pair(xs, 0), pair(xr, 0)), (pair(ys, 0), pair(yr, 0))
    x1, y1 = (pair(xs, pl.ds(1, 3)), pair(xr, pl.ds(1, 3))), (pair(ys, pl.ds(1, 3)), pair(yr, pl.ds(1, 3)))
    x2, y2 = (pair(xe), pair(xer)), (pair(ye), pair(yer))

    lane = lax.broadcasted_iota(jnp.int32, (8, lanes), 1)
    odd = lax.rem(lane, 2) == 1
    lane_r = lax.broadcasted_iota(jnp.int32, (ROWS, lanes), 1)
    first_lane, last_lane = lane_r == 0, lane_r == lanes - 1
    outer_lane = jnp.logical_or(first_lane, last_lane)
    zero8 = jnp.zeros((8, lanes), f32)

    def pack(values, slot, packs):
        turned = pltpu.roll(values, slot, 1)
        low = jnp.where(lane == slot, turned, packs[0])
        return low, jnp.where(lane == lax.rem(slot + lanes - 1, lanes), turned, packs[1])

    def keep(ref, packs, *at):
        ref[(0, *at)] = packs[0]
        ref[(1, *at)] = pltpu.roll(packs[1], 1, 1)

    def pack_rows(values, z, row, packs):
        for g in range(values.shape[0] // 8):
            packs = pack(values[8 * g:8 * g + 8, :], z * groups + row // 8 + g, packs)
        return packs

    def weave(low, high):
        low = pltpu.roll(low, 1, 1)
        return jnp.where(odd, low, high), jnp.where(odd, high, low)

    def ends_at(woven, z, row):
        parts = []
        for g in range(ROWS // 8):
            slot = z * groups + row // 8 + g
            parts.append(pltpu.roll(woven[(row // 8 + g) % 2], lanes - 1 - slot, 1))
        return jnp.concatenate(parts, axis=0)

    def yshift(v, ends):
        below, above = pltpu.roll(v, 1, 1), pltpu.roll(v, lanes - 1, 1)
        return jnp.where(first_lane, ends, below), jnp.where(last_lane, ends, above)

    fields = [u.at[0], u.at[1], u.at[2], p]

    def pack_field(i, n):
        def step(z, packs):
            return pack_rows(fields[i][z + 1, PAD:last, :], z, 0, packs)

        keep(ys, loop(step, (zero8, zero8)), n)

    def take_rows(i):
        def step(z, carry):
            xs[0, i, pl.ds(z, 1), :] = fields[i][z + 1, PAD:PAD + 1, :]
            xs[1, i, pl.ds(z, 1), :] = fields[i][z + 1, last - 1:last, :]
            return carry

        loop(step, 0)

    loads[0].wait()
    pack_field(1, 0)
    loads[1].wait()
    take_rows(0)
    pl.semaphore_wait(barrier, partners)
    send(ZU, "gz", zu)
    send(X0, "gx", x0)
    send(Y0, "gy", y0)
    send(ZB, "gz", zl, zq, zz)

    loads[2].wait()
    loads[3].wait()
    for i in range(1, 4):
        take_rows(i)
    pack_field(0, 1)
    pack_field(2, 2)
    pack_field(3, 3)
    send(X1, "gx", x1)
    send(Y1, "gy", y1)

    clear("gx", [[ref.at[side] for ref in (xr, xer)] for side in (0, 1)])
    clear("gy", [[ref.at[side] for ref in (yr, yer)] for side in (0, 1)])
    edges = (0, depth + 1)
    clear("gz", [[u.at[:, z, own], p.at[z, own], s.at[z], zn.at[z]] for z in edges])
    for axis, ref in (("gx", txr), ("gy", tyr)):
        for side in (0, 1):
            for off in far:
                @pl.when(jnp.logical_not(both(axis, side, off)))
                def _():
                    ref[side, off - 1] = jnp.zeros(ref.shape[2:], f32)

    for load in loads[4:]:
        load.wait()
    base = me["gz"] * depth

    inverse = [1.0 / jnp.full((8, lanes), tab[i], f32) for i in range(ZONES)]

    def rows_resistance(zones, active):
        count = zones.shape[0] // 8
        least = jnp.concatenate([inverse[0]] * count, axis=0)
        for i in range(1, ZONES):
            least = jnp.where(zones == i, jnp.concatenate([inverse[i]] * count, axis=0), least)
        return jnp.where(active, least * (1.0 / (0.001 + 0.999)), least * (1.0 / 0.001))

    def zone_step(z, packs):
        for row in chunks:
            zones = zn[z + 1, row:row + ROWS, :]
            ip[z, row:row + ROWS, :] = rows_resistance(zones, base + z < th[row:row + ROWS, :])
            packs = pack_rows(zones, z, row, packs)
        zr[0, pl.ds(z, 1), :] = zn[z + 1, 0:1, :]
        zr[1, pl.ds(z, 1), :] = zn[z + 1, width - 1:width, :]
        return packs

    none8 = jnp.zeros((8, lanes), jnp.int32)
    keep(zp, loop(zone_step, (none8, none8)))

    def spread(packs):
        step = groups
        while step < lanes:
            turned = [pltpu.roll(x, step, 1) for x in packs]
            packs = [x + y for x, y in zip(packs, turned)]
            step *= 2
        return packs

    edge_height = pack_rows(th[...], 0, 0, (none8, none8))
    edge_height = spread([edge_height[0], pltpu.roll(edge_height[1], 1, 1)])
    edge_layer = base + lane // groups

    for row in chunks:
        rows = slice(row, row + ROWS)
        at = slice(PAD + row, PAD + row + ROWS)

        def partial_step(z, carry, bottom=False, top=False):
            v = u[1, z + 1, at, :]
            ym, yp = pltpu.roll(v, 1, 1), pltpu.roll(v, lanes - 1, 1)
            div = jnp.where(last_lane, 0.0, yp) - jnp.where(first_lane, 0.0, ym)
            if not top:
                div = div + u[2, z + 2, at, :]
            if not bottom:
                div = div - u[2, z, at, :]
            t[z, at, :] = div
            return carry

        partial_step(0, 0, bottom=True)
        loop(partial_step, 0, 1, depth - 1)
        partial_step(depth - 1, 0, top=True)

    receive(ZU, "gz", lambda n: ip.at[pl.ds(0, n)])
    receive(X0, "gx", lambda n: xr.at[pl.ds(0, n), 0])
    receive(Y0, "gy", lambda n: yr.at[pl.ds(0, n), 0])

    def unpack_first(z, carry):
        u[0, z + 1, PAD - 1:PAD, :] = xr[0, 0, pl.ds(z, 1), :]
        u[0, z + 1, last:last + 1, :] = xr[1, 0, pl.ds(z, 1), :]
        return carry

    loop(unpack_first, 0)

    woven = weave(-yr[0, 0], yr[1, 0])

    def strain_of(z, row, bottom=False, top=False):
        at = slice(PAD + row, PAD + row + ROWS)
        up = u[0, z + 1, PAD + row + 1:PAD + row + 1 + ROWS, :]
        down = u[0, z + 1, PAD + row - 1:PAD + row - 1 + ROWS, :]
        div = t[z, at, :] + (up - down) + jnp.where(outer_lane, ends_at(woven, z, row), 0.0)
        if bottom:
            div = div - u[2, 0, at, :]
        if top:
            div = div + u[2, depth + 1, at, :]
        return 0.3 * jnp.tanh(0.5 * div)

    for row in chunks:
        s[1, row:row + ROWS, :] = strain_of(0, row, bottom=True)
        s[depth, row:row + ROWS, :] = strain_of(depth - 1, row, top=True)
    send(ZS, "gz", zs)
    for row in chunks:
        rows = slice(row, row + ROWS)
        height = th[rows, :]

        def strain_step(z, acc, outer=False):
            st = s[z + 1, rows, :] if outer else strain_of(z, row)
            if not outer:
                s[z + 1, rows, :] = st
            if row == 0:
                xe[0, 0, pl.ds(z, 1), :] = st[0:1, :]
            if row + ROWS == width:
                xe[1, 0, pl.ds(z, 1), :] = st[ROWS - 1:ROWS, :]
            acc = acc + jnp.where(base + z < height, 1.0 + st, 0.0)
            pre[z, rows, :] = acc
            return acc

        acc = strain_step(0, jnp.zeros((ROWS, lanes), f32), outer=True)
        acc = loop(strain_step, acc, 1, depth - 1)
        tot[rows, :] = strain_step(depth - 1, acc, outer=True)

    def column(off, at):
        return pltpu.make_async_remote_copy(
            src_ref=tot,
            dst_ref=cs.at[off - 1],
            send_sem=col_send.at[0],
            recv_sem=col_recv.at[0],
            device_id=round_z(at),
            device_id_type=MESH,
        )

    for side, row in ((0, 0), (1, width - 1)):
        tx[side] = tot[row:row + 1, :]
    keep(ty, pack_rows(tot[...], 0, 0, (zero8, zero8)))

    def edge_wait(sems, places):
        for i, (axis, ref) in enumerate((("gx", tall_x), ("gy", tall_y))):
            for n in sorted({a * b for a in (1, 2) for b in far}):
                @pl.when(sides_of(axis) * places == n)
                def _():
                    some = ref.at[pl.ds(0, n)]
                    pltpu.make_async_copy(some, some, sems.at[i]).wait()

    def start_edges(n):
        off = me["gz"] - n
        for i, (axis, src, dst) in enumerate((("gx", tx, txr), ("gy", ty, tyr))):
            for side in (0, 1):
                @pl.when(jnp.logical_and(has(axis, side), off > 0))
                def _():
                    pltpu.make_async_remote_copy(
                        src_ref=src.at[side],
                        dst_ref=dst.at[1 - side, off - 1],
                        send_sem=edge_send.at[i],
                        recv_sem=edge_recv.at[i],
                        device_id=peer(axis, side, -off),
                        device_id_type=MESH,
                    ).start()

    def start_column(n):
        target = n + (n >= me["gz"]).astype(jnp.int32)
        ahead = lax.rem(target - me["gz"] + size["gz"], size["gz"])
        column(ahead, ahead).start()

    if far:
        start_edges(0)
        start_column(0)

    packs = loop(lambda z, packs: pack_rows(s[z + 1], z, 0, packs), (zero8, zero8))
    edge = packs[0], pltpu.roll(packs[1], 1, 1)
    actives = [edge_layer < edge_height[side] for side in (0, 1)]
    thicknesses = [jnp.where(actives[side], 1.0 + edge[side], 0.0) for side in (0, 1)]
    aboves, step = thicknesses, groups
    while step < lanes:
        turned = [pltpu.roll(x, lanes - step, 1) for x in aboves]
        aboves = [x + jnp.where(lane < lanes - step, y, 0.0) for x, y in zip(aboves, turned)]
        step *= 2
    for side in (0, 1):
        st, active, thickness = edge[side], actives[side], thicknesses[side]
        h = 1.0 + st
        ye[side, 0] = st
        ye[side, 1] = 1.0 + scale * (aboves[side] - thickness)
        ye[side, 2] = rows_resistance(zp[side], active) / (h * h * h)
        row = (width - 1) * side

        def row_step(z, carry):
            xe[side, 1, pl.ds(z, 1), :] = 1.0 + scale * (tot[row:row + 1, :] - pre[z, row:row + 1, :])
            return carry

        loop(row_step, 0)
        h = 1.0 + xe[side, 0]
        layer = base + lax.broadcasted_iota(jnp.int32, (depth, lanes), 0)
        xe[side, 2] = rows_resistance(zr[side], layer < th[row:row + 1, :]) / (h * h * h)

    for n in far[1:]:
        start_edges(n - 1)
        start_column(n - 1)
    send(X2, "gx", x2)
    send(Y2, "gy", y2)

    receive(X1, "gx", lambda n: xr.at[pl.ds(0, n), pl.ds(1, 3)])
    receive(Y1, "gy", lambda n: yr.at[pl.ds(0, n), pl.ds(1, 3)])

    def gradient_step(z, carry):
        t[z, PAD:last, :] = 0.25 * s[z + 1] - 0.5 * p[z + 1, PAD:last, :]
        return carry

    loop(gradient_step, 0)

    def unpack_inputs(z, carry):
        for side, at in ((0, PAD - 1), (1, last)):
            for i in (1, 2):
                fields[i][z + 1, at:at + 1, :] = xr[side, i, pl.ds(z, 1), :]
            t[z, at:at + 1, :] = -0.5 * xr[side, 3, pl.ds(z, 1), :]
        return carry

    loop(unpack_inputs, 0)

    wovens = [weave(yr[0, n], yr[1, n]) for n in (1, 0, 2)]
    for row in chunks:
        rows = slice(row, row + ROWS)
        at = slice(PAD + row, PAD + row + ROWS)
        up1 = slice(PAD + row + 1, PAD + row + 1 + ROWS)
        down1 = slice(PAD + row - 1, PAD + row - 1 + ROWS)
        height = tot[rows, :]

        def inner_step(z, below, bottom=False, top=False):
            mids = [u[c, z + 1, at, :] for c in range(3)]
            pm, st, tm = p[z + 1, at, :], s[z + 1, rows, :], t[z, at, :]
            above = None
            if not top:
                twice = 2.0 / (2.0 + st + s[z + 2, rows, :])
                above = [twice * (u[c, z + 2, at, :] - mids[c]) for c in range(3)]
                gz[z + 1, rows, :] = 2.0 * twice * (p[z + 2, at, :] - pm)
            tb, ta = pltpu.roll(tm, 1, 1), pltpu.roll(tm, lanes - 1, 1)
            grads = [
                t[z, up1, :] - t[z, down1, :],
                jnp.where(last_lane, 0.0, ta) - jnp.where(first_lane, 0.0, tb),
            ]
            if bottom:
                grads.append(t[z + 1, at, :])
            elif top:
                grads.append(-t[z - 1, at, :])
            else:
                grads.append(t[z + 1, at, :] - t[z - 1, at, :])
            for c in range(3):
                ym, yp = yshift(mids[c], ends_at(wovens[c], z, row))
                out = u[c, z + 1, up1, :] + u[c, z + 1, down1, :] + ym + yp - 4.0 * mids[c] + grads[c]
                if not top:
                    out = out + above[c]
                if not bottom:
                    out = out - below[c]
                mech[c, z, rows, :] = out
            gx[z, rows, :] = 2.0 * (p[z + 1, up1, :] - pm)
            gy[z, rows, :] = jnp.where(last_lane, 0.0, 2.0 * (pltpu.roll(pm, lanes - 1, 1) - pm))
            h = 1.0 + st
            free = ip[z, rows, :] / (h * h * h)
            inv[z + 1, rows, :] = free
            r[z + 1, rows, :] = free + (scale * (height - pre[z, rows, :])) * free
            return tuple(above) if above else None

        below = inner_step(0, None, bottom=True)
        below = loop(lambda z, b: inner_step(z, b), below, 1, depth - 1)
        inner_step(depth - 1, below, top=True)

    receive(ZB, "gz", lambda n: ip.at[pl.ds(0, 4 * n)])
    receive(ZS, "gz", lambda n: ip.at[pl.ds(0, n)])

    for row in chunks:
        rows = slice(row, row + ROWS)
        at = slice(PAD + row, PAD + row + ROWS)
        for side, z, halo in ((0, 0, 0), (1, depth - 1, depth + 1)):
            sign = 1.0 if side else -1.0
            st = s[halo, rows, :]
            twice = 2.0 / (2.0 + s[z + 1, rows, :] + st)
            for c in range(3):
                out = mech[c, z, rows, :] + twice * (u[c, halo, at, :] - u[c, z + 1, at, :])
                if c == 2:
                    out = out + sign * (0.25 * st - 0.5 * p[halo, at, :])
                mech[c, z, rows, :] = out
            gz[z + side, rows, :] = (2.0 * sign * mask("gz", side)) * (twice * (p[halo, at, :] - p[z + 1, at, :]))
            active = base + halo - 1 < th[rows, :]
            h = 1.0 + st
            free = rows_resistance(zn[halo, rows, :], active) / (h * h * h)
            part = jnp.where(active, -h, 0.0) if side else tot[rows, :]
            r[halo, rows, :] = free + (scale * part) * free
            inv[halo, rows, :] = free

    receive(X2, "gx", lambda n: xer.at[pl.ds(0, n)])
    receive(Y2, "gy", lambda n: yer.at[pl.ds(0, n)])

    def side_rows(z, carry):
        for side, x in ((0, 0), (1, width - 1)):
            step = (0.25 if side else -0.25) * xer[side, 0, pl.ds(z, 1), :]
            mech[0, z, x:x + 1, :] = mech[0, z, x:x + 1, :] + step
        return carry

    loop(side_rows, 0)
    for side in (0, 1):
        sign = 1.0 if side else -1.0
        gxe[side] = (2.0 * sign * mask("gx", side)) * (xr[side, 3] - xs[side, 3])
        gye[side] = (2.0 * mask("gy", side)) * (yr[side, 3] - ys[side, 3])
    woven = weave(-(0.25 * yer[0, 0] - 0.5 * yr[0, 3]), 0.25 * yer[1, 0] - 0.5 * yr[1, 3])

    def side_lanes(z, carry):
        for row in chunks:
            rows = slice(row, row + ROWS)
            mech[1, z, rows, :] = mech[1, z, rows, :] + jnp.where(outer_lane, ends_at(woven, z, row), 0.0)
        return carry

    loop(side_lanes, 0)

    every = ip.at[pl.ds(0, size["gz"] - 1)]
    pltpu.make_async_copy(every, every, col_recv.at[0]).wait()
    edge_wait(edge_recv, size["gz"] - 1 - me["gz"])

    finished(side_send.at[0], "gx", lambda n: inv.at[pl.ds(0, 7 * n), pl.ds(0, depth)])
    finished(side_send.at[1], "gy", lambda n: inv.at[pl.ds(0, 7 * n), pl.ds(0, 8)])
    finished(side_send.at[2], "gz", lambda n: inv.at[pl.ds(0, 6 * n)])
    pltpu.make_async_copy(every, every, col_send.at[0]).wait()
    edge_wait(edge_send, me["gz"])


def finish(
    counts, pre, cs, part, inv, gx, gy, gz, s, mech, gxe, gye, xe, xer, ye, yer, txr, tyr,
    heights_out, flow_out, mech_out, heights, flow, fx, fy, r, rows_in, upper, sem,
):
    depth, width, lanes = pre.shape
    groups = width // 8
    f32 = jnp.float32
    depth_total = depth * counts[2]
    scale = 2.0 / depth_total
    stores = [pltpu.make_async_copy(mech, mech_out, sem.at[0]), pltpu.make_async_copy(heights, heights_out, sem.at[1])]
    stores[0].start()
    lane = lax.broadcasted_iota(jnp.int32, (ROWS, lanes), 1)
    outer = jnp.logical_or(lane == 0, lane == lanes - 1)
    lane8 = lax.broadcasted_iota(jnp.int32, (8, lanes), 1)
    chunks = range(0, width, ROWS)
    far = range(1, counts[2])
    place = lax.axis_index("gz")

    below, above = jnp.zeros((width, lanes), f32), jnp.zeros((width, lanes), f32)
    for off in far:
        piece = cs[off - 1]
        low = (place >= off).astype(f32)
        below = below + piece * low
        above = above + piece * (1.0 - low)
    below = below * (1.0 / depth_total)
    above = scale * above
    upper[...] = above
    for z in range(depth):
        heights[z] = pre[z] * (1.0 / depth_total) + below
    stores[1].start()
    low, high = jnp.zeros((8, lanes), f32), jnp.zeros((8, lanes), f32)
    for g in range(groups):
        values = above[8 * g:8 * g + 8, :]
        low = jnp.where(lane8 == g, pltpu.roll(values, g, 1), low)
        high = jnp.where(lane8 == g, pltpu.roll(values, g + 1, 1), high)
    packed = [low, high]
    for side in (0, 1):
        beyond = jnp.zeros((8, lanes), f32)
        for off in far:
            beyond = beyond + scale * tyr[side, off - 1]
        packed.append(beyond)
    step = groups
    while step < lanes:
        turned = [pltpu.roll(x, step, 1) for x in packed]
        packed = [x + y for x, y in zip(packed, turned)]
        step *= 2
    ends = []
    for side, end in ((0, above[0:1, :]), (1, above[width - 1:width, :])):
        here = (ye[side, 1] + packed[side]) * ye[side, 2]
        there = (yer[side, 1] + packed[2 + side]) * yer[side, 2]
        ends.append(gye[side] / (here + there))
        beyond = jnp.zeros((1, lanes), f32)
        for off in far:
            beyond = beyond + scale * txr[side, off - 1]
        here = (xe[side, 1] + end) * xe[side, 2]
        there = (xer[side, 1] + beyond) * xer[side, 2]
        rows_in[side] = gxe[side] / (here + there)
    odd = lax.rem(lane8, 2) == 1
    first_end = pltpu.roll(ends[0], 1, 1)
    flow_woven = jnp.where(odd, first_end, ends[1]), jnp.where(odd, ends[1], first_end)

    def resist(z, carry):
        r[z, 0:width, :] = part[z] + upper[...] * inv[z]
        return carry

    lax.fori_loop(0, depth + 2, resist, 0, unroll=depth + 2)

    def sides(woven, z, row):
        tiles = []
        for g in range(ROWS // 8):
            slot = z * groups + row // 8 + g
            tiles.append(pltpu.roll(woven[(row // 8 + g) % 2], lanes - 1 - slot, 1))
        return jnp.where(outer, jnp.concatenate(tiles, axis=0), 0.0)

    def rise(z, rows):
        return gz[z, rows, :] / (r[z, rows, :] + r[z + 1, rows, :])

    def lateral(z, carry):
        fx[z, PAD - 1:PAD, :] = rows_in[0, pl.ds(z, 1), :]
        mid = r[z + 1, 0:width, :]
        fy[z] = gy[z] / (mid + pltpu.roll(mid, lanes - 1, 1))
        fx[z, PAD:PAD + width, :] = gx[z] / (mid + r[z + 1, 1:width + 1, :])
        fx[z, PAD + width - 1:PAD + width, :] = rows_in[1, pl.ds(z, 1), :]
        return carry

    def step_z(z, carry):
        out = []
        for row, under in zip(chunks, carry):
            rows = slice(row, row + ROWS)
            over = rise(z + 1, rows)
            face = fy[z, rows, :]
            total = (over - under) + (face - pltpu.roll(face, 1, 1)) - s[z + 1, rows, :]
            total = total + (fx[z, PAD + row:PAD + row + ROWS, :] - fx[z, PAD + row - 1:PAD + row - 1 + ROWS, :])
            flow[z, rows, :] = total + sides(flow_woven, z, row)
            out.append(over)
        return tuple(out)

    carry = tuple(rise(0, slice(row, row + ROWS)) for row in chunks)
    parts = 4 if depth % 4 == 0 else 1
    some = depth // parts
    for n in range(parts):
        span = n * some, (n + 1) * some
        lax.fori_loop(*span, lateral, 0, unroll=some)
        carry = lax.fori_loop(*span, step_z, carry, unroll=some)
        layers = pl.ds(n * some, some)
        pltpu.make_async_copy(flow.at[layers], flow_out.at[layers], sem.at[2]).start()
    pltpu.make_async_copy(flow, flow_out, sem.at[2]).wait()
    for copy in stores:
        copy.wait()


def local(counts, displacement, pressure, zone, perm_table, thickness):
    _, depth, width, lanes = displacement.shape
    f32, i32 = jnp.float32, jnp.int32
    tall = (depth + 2, width + 2 * PAD, lanes)
    cells, plane = (depth, width, lanes), (width, lanes)
    hbm, vmem = (pl.BlockSpec(memory_space=m) for m in (pl.ANY, pltpu.VMEM))
    far = max(counts[2] - 1, 1)
    V = lambda *shape, dtype=f32: pltpu.VMEM(shape, dtype)
    D = pltpu.SemaphoreType.DMA
    inputs = [
        pltpu.with_memory_space_constraint(x, pltpu.HBM)
        for x in (displacement, pressure, zone, perm_table, thickness)
    ]
    layers = (depth + 2, width, lanes)
    rows, packs = (depth, lanes), (8, lanes)
    results = (
        V(*cells), V(far, *plane), V(*layers), V(*layers), V(*cells), V(*cells), V(depth + 1, *plane), V(*layers),
        V(3, *cells), V(2, *rows), V(2, *packs), V(2, 3, *rows), V(2, 3, *rows), V(2, 3, *packs), V(2, 3, *packs),
        V(2, far, 1, lanes), V(2, far, *packs),
    )
    fields = pl.pallas_call(
        functools.partial(kernel, counts),
        out_shape=results,
        in_specs=[hbm] * 5,
        out_specs=(vmem,) * len(results),
        scratch_shapes=[
            V(3, *tall), V(*tall), V(depth, width + 2 * PAD, lanes), V(*layers, dtype=i32), V(*plane, dtype=i32),
            pltpu.SMEM((ZONES,), f32), V(*cells), V(*plane), V(2, 4, *rows), V(2, 4, *rows), V(2, 4, *packs), V(2, 4, *packs),
            V(2, *rows, dtype=i32), V(2, *packs, dtype=i32), V(2, 1, lanes), V(2, *packs),
            V(2 * far, 1, lanes), V(2 * far, *packs), D((7,)), D((9,)), D((3,)), D((1,)), D((1,)), D((2,)), D((2,)),
        ],
        compiler_params=pltpu.CompilerParams(
            collective_id=0, has_side_effects=True, vmem_limit_bytes=40 * 2**20
        ),
    )(*inputs)
    return pl.pallas_call(
        functools.partial(finish, counts),
        out_shape=tuple(jax.ShapeDtypeStruct(x.shape, f32) for x in (pressure, pressure, displacement)),
        in_specs=[vmem] * len(results),
        out_specs=(hbm,) * 3,
        scratch_shapes=[
            V(*cells), V(*cells), V(depth, width + 2 * PAD, lanes), V(*cells), V(depth + 2, width + 8, lanes),
            V(2, *rows), V(*plane), D((3,)),
        ],
        compiler_params=pltpu.CompilerParams(vmem_limit_bytes=8 * 2**20),
    )(*[pltpu.with_memory_space_constraint(x, pltpu.VMEM) for x in fields])


def solution(mesh):
    counts = tuple(mesh.shape[axis] for axis in AXES)
    in_specs = (
        P(None, "gz", "gx", "gy"),
        P("gz", "gx", "gy"),
        P("gz", "gx", "gy"),
        P(),
        P("gx", "gy"),
    )
    out_specs = (P("gz", "gx", "gy"), P("gz", "gx", "gy"), P(None, "gz", "gx", "gy"))
    return jax.shard_map(
        functools.partial(local, counts), mesh=mesh, in_specs=in_specs, out_specs=out_specs, check_vma=False
    )
```

```python
import functools

import jax
import jax.numpy as jnp
from jax import lax
from jax.experimental import pallas as pl
from jax.experimental.pallas import tpu as pltpu
from jax.sharding import PartitionSpec as P

MESH = pl.DeviceIdType.MESH
ZONES = 8
AXES = ("gx", "gy", "gz")
PAD = 8
ROWS = 32
WIDE = 64

ZU, ZB, X0, Y0, X1, Y1, ZS, X2, Y2 = range(9)


def kernel(
    counts, disp, press, zone, table, thick,
    pre, cs, r, inv, gx, gy, gz, s, mech, gxe, gye, xe, xer, ye, yer, txr, tyr,
    u, p, t, zn, th, tab, ip, tot, xs, xr, ys, yr, zr, zp, tx, ty, tall_x, tall_y,
    load_sem, recv_sem, side_send, col_send, col_recv, edge_send, edge_recv,
):
    depth, width, lanes = press.shape
    groups = width // 8
    last = PAD + width
    me = {axis: lax.axis_index(axis) for axis in AXES}
    size = dict(zip(AXES, counts))
    depth_total = depth * size["gz"]
    scale = 2.0 / depth_total
    own = pl.ds(PAD, width)
    f32 = jnp.float32
    chunks = range(0, width, ROWS)
    far = range(1, size["gz"])

    def has(axis, side):
        return me[axis] > 0 if side == 0 else me[axis] < size[axis] - 1

    def mask(axis, side):
        return has(axis, side).astype(f32)

    def peer(axis, side, up=None):
        place = {axis: me[axis] + (1 if side else -1)}
        if up is not None:
            place["gz"] = me["gz"] + up
        return place

    def round_z(off):
        return {"gz": lax.rem(me["gz"] + off, size["gz"])}

    def both(axis, side, off):
        inside = me["gz"] + off < size["gz"] if off > 0 else me["gz"] + off >= 0
        return jnp.logical_and(has(axis, side), inside)

    def loop(step, carry, start=0, end=depth):
        return lax.fori_loop(start, end, step, carry, unroll=end - start)

    inner = pl.ds(1, depth)
    loads = [
        pltpu.make_async_copy(disp.at[1], u.at[1, inner, own], load_sem.at[0]),
        pltpu.make_async_copy(disp.at[0], u.at[0, inner, own], load_sem.at[1]),
        pltpu.make_async_copy(disp.at[2], u.at[2, inner, own], load_sem.at[2]),
        pltpu.make_async_copy(press, p.at[inner, own], load_sem.at[3]),
        pltpu.make_async_copy(zone, zn.at[inner], load_sem.at[4]),
        pltpu.make_async_copy(thick, th, load_sem.at[5]),
        pltpu.make_async_copy(table, tab, load_sem.at[6]),
    ]
    loads[0].start()

    barrier = pltpu.get_barrier_semaphore()
    partners = jnp.int32(size["gz"] - 1)
    for axis in ("gx", "gy"):
        for side in (0, 1):
            @pl.when(has(axis, side))
            def _():
                pl.semaphore_signal(barrier, inc=1, device_id=peer(axis, side), device_id_type=MESH)
            partners = partners + has(axis, side).astype(jnp.int32) * (1 + me["gz"])
    for off in far:
        pl.semaphore_signal(barrier, inc=1, device_id=round_z(off), device_id_type=MESH)
    for load in loads[1:]:
        load.start()
    for axis in ("gx", "gy"):
        for side in (0, 1):
            for off in far:
                @pl.when(both(axis, side, off))
                def _():
                    pl.semaphore_signal(barrier, inc=1, device_id=peer(axis, side, off), device_id_type=MESH)

    def copy(message, axis, side, src, dst, at):
        return pltpu.make_async_remote_copy(
            src_ref=src,
            dst_ref=dst,
            send_sem=side_send.at[AXES.index(axis)],
            recv_sem=recv_sem.at[message],
            device_id=peer(axis, at),
            device_id_type=MESH,
        )

    def send(message, axis, *parts):
        for side in (0, 1):
            @pl.when(has(axis, side))
            def _():
                for srcs, dsts in parts:
                    copy(message, axis, side, srcs[side], dsts[1 - side], side).start()

    def sides_of(axis):
        return has(axis, 0).astype(jnp.int32) + has(axis, 1).astype(jnp.int32)

    def finished(sem, axis, part):
        for n in (1, 2):
            @pl.when(sides_of(axis) == n)
            def _():
                pltpu.make_async_copy(part(n), part(n), sem).wait()

    def receive(message, axis, part):
        finished(recv_sem.at[message], axis, part)

    def clear(axis, refs):
        for side in (0, 1):
            @pl.when(jnp.logical_not(has(axis, side)))
            def _():
                for ref in refs[side]:
                    ref[...] = jnp.zeros(ref.shape, ref.dtype)

    def pair(ref, *at):
        return (ref.at[(0, *at)], ref.at[(1, *at)])

    zu = ((disp.at[2, 0], disp.at[2, depth - 1]), (u.at[2, 0, own], u.at[2, depth + 1, own]))
    zl = (
        (disp.at[pl.ds(0, 2), 0], disp.at[pl.ds(0, 2), depth - 1]),
        (u.at[pl.ds(0, 2), 0, own], u.at[pl.ds(0, 2), depth + 1, own]),
    )
    zq = ((press.at[0], press.at[depth - 1]), (p.at[0, own], p.at[depth + 1, own]))
    zz = ((zone.at[0], zone.at[depth - 1]), (zn.at[0], zn.at[depth + 1]))
    zs = ((s.at[1], s.at[depth]), (s.at[0], s.at[depth + 1]))
    x0, y0 = (pair(xs, 0), pair(xr, 0)), (pair(ys, 0), pair(yr, 0))
    x1, y1 = (pair(xs, pl.ds(1, 3)), pair(xr, pl.ds(1, 3))), (pair(ys, pl.ds(1, 3)), pair(yr, pl.ds(1, 3)))
    x2, y2 = (pair(xe), pair(xer)), (pair(ye), pair(yer))

    lane = lax.broadcasted_iota(jnp.int32, (8, lanes), 1)
    odd = lax.rem(lane, 2) == 1
    lane_r = lax.broadcasted_iota(jnp.int32, (ROWS, lanes), 1)
    first_lane, last_lane = lane_r == 0, lane_r == lanes - 1
    outer_lane = jnp.logical_or(first_lane, last_lane)
    zero8 = jnp.zeros((8, lanes), f32)

    def pack(values, slot, packs):
        turned = pltpu.roll(values, slot, 1)
        low = jnp.where(lane == slot, turned, packs[0])
        return low, jnp.where(lane == lax.rem(slot + lanes - 1, lanes), turned, packs[1])

    def keep(ref, packs, *at):
        ref[(0, *at)] = packs[0]
        ref[(1, *at)] = pltpu.roll(packs[1], 1, 1)

    def pack_rows(values, z, row, packs):
        for g in range(values.shape[0] // 8):
            packs = pack(values[8 * g:8 * g + 8, :], z * groups + row // 8 + g, packs)
        return packs

    def weave(low, high):
        low = pltpu.roll(low, 1, 1)
        return jnp.where(odd, low, high), jnp.where(odd, high, low)

    def ends_at(woven, z, row):
        parts = []
        for g in range(ROWS // 8):
            slot = z * groups + row // 8 + g
            parts.append(pltpu.roll(woven[(row // 8 + g) % 2], lanes - 1 - slot, 1))
        return jnp.concatenate(parts, axis=0)

    def yshift(v, ends):
        below, above = pltpu.roll(v, 1, 1), pltpu.roll(v, lanes - 1, 1)
        return jnp.where(first_lane, ends, below), jnp.where(last_lane, ends, above)

    fields = [u.at[0], u.at[1], u.at[2], p]

    def pack_field(i, n):
        def step(z, packs):
            return pack_rows(fields[i][z + 1, PAD:last, :], z, 0, packs)

        keep(ys, loop(step, (zero8, zero8)), n)

    def take_rows(i):
        def step(z, carry):
            xs[0, i, pl.ds(z, 1), :] = fields[i][z + 1, PAD:PAD + 1, :]
            xs[1, i, pl.ds(z, 1), :] = fields[i][z + 1, last - 1:last, :]
            return carry

        loop(step, 0)

    loads[0].wait()
    pack_field(1, 0)
    loads[1].wait()
    take_rows(0)
    pl.semaphore_wait(barrier, partners)
    send(ZU, "gz", zu)
    send(X0, "gx", x0)
    send(Y0, "gy", y0)
    send(ZB, "gz", zl, zq, zz)

    loads[2].wait()
    loads[3].wait()
    for i in range(1, 4):
        take_rows(i)
    pack_field(0, 1)
    pack_field(2, 2)
    pack_field(3, 3)
    send(X1, "gx", x1)
    send(Y1, "gy", y1)

    clear("gx", [[ref.at[side] for ref in (xr, xer)] for side in (0, 1)])
    clear("gy", [[ref.at[side] for ref in (yr, yer)] for side in (0, 1)])
    edges = (0, depth + 1)
    clear("gz", [[u.at[:, z, own], p.at[z, own], s.at[z], zn.at[z]] for z in edges])
    for axis, ref in (("gx", txr), ("gy", tyr)):
        for side in (0, 1):
            for off in far:
                @pl.when(jnp.logical_not(both(axis, side, off)))
                def _():
                    ref[side, off - 1] = jnp.zeros(ref.shape[2:], f32)

    for load in loads[4:]:
        load.wait()
    base = me["gz"] * depth

    inverse = [1.0 / jnp.full((8, lanes), tab[i], f32) for i in range(ZONES)]

    def rows_resistance(zones, active):
        count = zones.shape[0] // 8
        least = jnp.concatenate([inverse[0]] * count, axis=0)
        for i in range(1, ZONES):
            least = jnp.where(zones == i, jnp.concatenate([inverse[i]] * count, axis=0), least)
        return jnp.where(active, least * (1.0 / (0.001 + 0.999)), least * (1.0 / 0.001))

    def zone_step(z, packs):
        for row in chunks:
            zones = zn[z + 1, row:row + ROWS, :]
            ip[z, row:row + ROWS, :] = rows_resistance(zones, base + z < th[row:row + ROWS, :])
            packs = pack_rows(zones, z, row, packs)
        zr[0, pl.ds(z, 1), :] = zn[z + 1, 0:1, :]
        zr[1, pl.ds(z, 1), :] = zn[z + 1, width - 1:width, :]
        return packs

    none8 = jnp.zeros((8, lanes), jnp.int32)
    keep(zp, loop(zone_step, (none8, none8)))

    def spread(packs):
        step = groups
        while step < lanes:
            turned = [pltpu.roll(x, step, 1) for x in packs]
            packs = [x + y for x, y in zip(packs, turned)]
            step *= 2
        return packs

    edge_height = pack_rows(th[...], 0, 0, (none8, none8))
    edge_height = spread([edge_height[0], pltpu.roll(edge_height[1], 1, 1)])
    edge_layer = base + lane // groups

    for row in chunks:
        rows = slice(row, row + ROWS)
        at = slice(PAD + row, PAD + row + ROWS)

        def partial_step(z, carry, bottom=False, top=False):
            v = u[1, z + 1, at, :]
            ym, yp = pltpu.roll(v, 1, 1), pltpu.roll(v, lanes - 1, 1)
            div = jnp.where(last_lane, 0.0, yp) - jnp.where(first_lane, 0.0, ym)
            if not top:
                div = div + u[2, z + 2, at, :]
            if not bottom:
                div = div - u[2, z, at, :]
            t[z, at, :] = div
            return carry

        partial_step(0, 0, bottom=True)
        loop(partial_step, 0, 1, depth - 1)
        partial_step(depth - 1, 0, top=True)

    receive(ZU, "gz", lambda n: ip.at[pl.ds(0, n)])
    receive(X0, "gx", lambda n: xr.at[pl.ds(0, n), 0])
    receive(Y0, "gy", lambda n: yr.at[pl.ds(0, n), 0])

    def unpack_first(z, carry):
        u[0, z + 1, PAD - 1:PAD, :] = xr[0, 0, pl.ds(z, 1), :]
        u[0, z + 1, last:last + 1, :] = xr[1, 0, pl.ds(z, 1), :]
        return carry

    loop(unpack_first, 0)

    woven = weave(-yr[0, 0], yr[1, 0])

    def strain_of(z, row, bottom=False, top=False):
        at = slice(PAD + row, PAD + row + ROWS)
        up = u[0, z + 1, PAD + row + 1:PAD + row + 1 + ROWS, :]
        down = u[0, z + 1, PAD + row - 1:PAD + row - 1 + ROWS, :]
        div = t[z, at, :] + (up - down) + jnp.where(outer_lane, ends_at(woven, z, row), 0.0)
        if bottom:
            div = div - u[2, 0, at, :]
        if top:
            div = div + u[2, depth + 1, at, :]
        return 0.3 * jnp.tanh(0.5 * div)

    for row in chunks:
        rows = slice(row, row + ROWS)
        height = th[rows, :]

        def strain_step(z, acc, bottom=False, top=False):
            st = strain_of(z, row, bottom, top)
            s[z + 1, rows, :] = st
            acc = acc + jnp.where(base + z < height, 1.0 + st, 0.0)
            pre[z, rows, :] = acc
            return acc

        acc = strain_step(0, jnp.zeros((ROWS, lanes), f32), bottom=True)
        acc = loop(strain_step, acc, 1, depth - 1)
        tot[rows, :] = strain_step(depth - 1, acc, top=True)

    def column(off, at):
        return pltpu.make_async_remote_copy(
            src_ref=tot,
            dst_ref=cs.at[off - 1],
            send_sem=col_send.at[0],
            recv_sem=col_recv.at[0],
            device_id=round_z(at),
            device_id_type=MESH,
        )

    for side, row in ((0, 0), (1, width - 1)):
        tx[side] = tot[row:row + 1, :]
    keep(ty, pack_rows(tot[...], 0, 0, (zero8, zero8)))

    def edge_wait(sems, places):
        for i, (axis, ref) in enumerate((("gx", tall_x), ("gy", tall_y))):
            for n in sorted({a * b for a in (1, 2) for b in far}):
                @pl.when(sides_of(axis) * places == n)
                def _():
                    some = ref.at[pl.ds(0, n)]
                    pltpu.make_async_copy(some, some, sems.at[i]).wait()

    def start_edges(n):
        off = me["gz"] - n
        for i, (axis, src, dst) in enumerate((("gx", tx, txr), ("gy", ty, tyr))):
            for side in (0, 1):
                @pl.when(jnp.logical_and(has(axis, side), off > 0))
                def _():
                    pltpu.make_async_remote_copy(
                        src_ref=src.at[side],
                        dst_ref=dst.at[1 - side, off - 1],
                        send_sem=edge_send.at[i],
                        recv_sem=edge_recv.at[i],
                        device_id=peer(axis, side, -off),
                        device_id_type=MESH,
                    ).start()

    def start_column(n):
        target = n + (n >= me["gz"]).astype(jnp.int32)
        ahead = lax.rem(target - me["gz"] + size["gz"], size["gz"])
        column(ahead, ahead).start()

    if far:
        start_edges(0)
        start_column(0)

    packs = loop(lambda z, packs: pack_rows(s[z + 1], z, 0, packs), (zero8, zero8))
    edge = packs[0], pltpu.roll(packs[1], 1, 1)
    actives = [edge_layer < edge_height[side] for side in (0, 1)]
    thicknesses = [jnp.where(actives[side], 1.0 + edge[side], 0.0) for side in (0, 1)]
    aboves, step = thicknesses, groups
    while step < lanes:
        turned = [pltpu.roll(x, lanes - step, 1) for x in aboves]
        aboves = [x + jnp.where(lane < lanes - step, y, 0.0) for x, y in zip(aboves, turned)]
        step *= 2
    for side in (0, 1):
        st, active, thickness = edge[side], actives[side], thicknesses[side]
        h = 1.0 + st
        ye[side, 0] = st
        ye[side, 1] = 1.0 + scale * (aboves[side] - thickness)
        ye[side, 2] = rows_resistance(zp[side], active) / (h * h * h)
        row = (width - 1) * side

        def row_step(z, carry):
            xe[side, 0, pl.ds(z, 1), :] = s[z + 1, row:row + 1, :]
            xe[side, 1, pl.ds(z, 1), :] = 1.0 + scale * (tot[row:row + 1, :] - pre[z, row:row + 1, :])
            return carry

        loop(row_step, 0)
        h = 1.0 + xe[side, 0]
        layer = base + lax.broadcasted_iota(jnp.int32, (depth, lanes), 0)
        xe[side, 2] = rows_resistance(zr[side], layer < th[row:row + 1, :]) / (h * h * h)

    for n in far[1:]:
        start_edges(n - 1)
        start_column(n - 1)
    send(ZS, "gz", zs)
    send(X2, "gx", x2)
    send(Y2, "gy", y2)

    receive(X1, "gx", lambda n: xr.at[pl.ds(0, n), pl.ds(1, 3)])
    receive(Y1, "gy", lambda n: yr.at[pl.ds(0, n), pl.ds(1, 3)])

    def gradient_step(z, carry):
        t[z, PAD:last, :] = 0.25 * s[z + 1] - 0.5 * p[z + 1, PAD:last, :]
        return carry

    loop(gradient_step, 0)

    def unpack_inputs(z, carry):
        for side, at in ((0, PAD - 1), (1, last)):
            for i in (1, 2):
                fields[i][z + 1, at:at + 1, :] = xr[side, i, pl.ds(z, 1), :]
            t[z, at:at + 1, :] = -0.5 * xr[side, 3, pl.ds(z, 1), :]
        return carry

    loop(unpack_inputs, 0)

    wovens = [weave(yr[0, n], yr[1, n]) for n in (1, 0, 2)]
    for row in chunks:
        rows = slice(row, row + ROWS)
        at = slice(PAD + row, PAD + row + ROWS)
        up1 = slice(PAD + row + 1, PAD + row + 1 + ROWS)
        down1 = slice(PAD + row - 1, PAD + row - 1 + ROWS)
        height = tot[rows, :]

        def inner_step(z, below, bottom=False, top=False):
            mids = [u[c, z + 1, at, :] for c in range(3)]
            pm, st, tm = p[z + 1, at, :], s[z + 1, rows, :], t[z, at, :]
            above = None
            if not top:
                twice = 2.0 / (2.0 + st + s[z + 2, rows, :])
                above = [twice * (u[c, z + 2, at, :] - mids[c]) for c in range(3)]
                gz[z + 1, rows, :] = 2.0 * twice * (p[z + 2, at, :] - pm)
            tb, ta = pltpu.roll(tm, 1, 1), pltpu.roll(tm, lanes - 1, 1)
            grads = [
                t[z, up1, :] - t[z, down1, :],
                jnp.where(last_lane, 0.0, ta) - jnp.where(first_lane, 0.0, tb),
            ]
            if bottom:
                grads.append(t[z + 1, at, :])
            elif top:
                grads.append(-t[z - 1, at, :])
            else:
                grads.append(t[z + 1, at, :] - t[z - 1, at, :])
            for c in range(3):
                ym, yp = yshift(mids[c], ends_at(wovens[c], z, row))
                out = u[c, z + 1, up1, :] + u[c, z + 1, down1, :] + ym + yp - 4.0 * mids[c] + grads[c]
                if not top:
                    out = out + above[c]
                if not bottom:
                    out = out - below[c]
                mech[c, z, rows, :] = out
            gx[z, rows, :] = 2.0 * (p[z + 1, up1, :] - pm)
            gy[z, rows, :] = jnp.where(last_lane, 0.0, 2.0 * (pltpu.roll(pm, lanes - 1, 1) - pm))
            h = 1.0 + st
            free = ip[z, rows, :] / (h * h * h)
            inv[z + 1, rows, :] = free
            r[z + 1, rows, :] = free + (scale * (height - pre[z, rows, :])) * free
            return tuple(above) if above else None

        below = inner_step(0, None, bottom=True)
        below = loop(lambda z, b: inner_step(z, b), below, 1, depth - 1)
        inner_step(depth - 1, below, top=True)

    receive(ZB, "gz", lambda n: ip.at[pl.ds(0, 4 * n)])
    receive(ZS, "gz", lambda n: ip.at[pl.ds(0, n)])

    for row in chunks:
        rows = slice(row, row + ROWS)
        at = slice(PAD + row, PAD + row + ROWS)
        for side, z, halo in ((0, 0, 0), (1, depth - 1, depth + 1)):
            sign = 1.0 if side else -1.0
            st = s[halo, rows, :]
            twice = 2.0 / (2.0 + s[z + 1, rows, :] + st)
            for c in range(3):
                out = mech[c, z, rows, :] + twice * (u[c, halo, at, :] - u[c, z + 1, at, :])
                if c == 2:
                    out = out + sign * (0.25 * st - 0.5 * p[halo, at, :])
                mech[c, z, rows, :] = out
            gz[z + side, rows, :] = (2.0 * sign * mask("gz", side)) * (twice * (p[halo, at, :] - p[z + 1, at, :]))
            active = base + halo - 1 < th[rows, :]
            h = 1.0 + st
            free = rows_resistance(zn[halo, rows, :], active) / (h * h * h)
            part = jnp.where(active, -h, 0.0) if side else tot[rows, :]
            r[halo, rows, :] = free + (scale * part) * free
            inv[halo, rows, :] = free

    receive(X2, "gx", lambda n: xer.at[pl.ds(0, n)])
    receive(Y2, "gy", lambda n: yer.at[pl.ds(0, n)])

    def side_rows(z, carry):
        for side, x in ((0, 0), (1, width - 1)):
            step = (0.25 if side else -0.25) * xer[side, 0, pl.ds(z, 1), :]
            mech[0, z, x:x + 1, :] = mech[0, z, x:x + 1, :] + step
        return carry

    loop(side_rows, 0)
    for side in (0, 1):
        sign = 1.0 if side else -1.0
        gxe[side] = (2.0 * sign * mask("gx", side)) * (xr[side, 3] - xs[side, 3])
        gye[side] = (2.0 * mask("gy", side)) * (yr[side, 3] - ys[side, 3])
    woven = weave(-(0.25 * yer[0, 0] - 0.5 * yr[0, 3]), 0.25 * yer[1, 0] - 0.5 * yr[1, 3])

    def side_lanes(z, carry):
        for row in chunks:
            rows = slice(row, row + ROWS)
            mech[1, z, rows, :] = mech[1, z, rows, :] + jnp.where(outer_lane, ends_at(woven, z, row), 0.0)
        return carry

    loop(side_lanes, 0)

    every = ip.at[pl.ds(0, size["gz"] - 1)]
    pltpu.make_async_copy(every, every, col_recv.at[0]).wait()
    edge_wait(edge_recv, size["gz"] - 1 - me["gz"])

    finished(side_send.at[0], "gx", lambda n: inv.at[pl.ds(0, 7 * n), pl.ds(0, depth)])
    finished(side_send.at[1], "gy", lambda n: inv.at[pl.ds(0, 7 * n), pl.ds(0, 8)])
    finished(side_send.at[2], "gz", lambda n: inv.at[pl.ds(0, 6 * n)])
    pltpu.make_async_copy(every, every, col_send.at[0]).wait()
    edge_wait(edge_send, me["gz"])


def finish(
    counts, pre, cs, part, inv, gx, gy, gz, s, mech, gxe, gye, xe, xer, ye, yer, txr, tyr,
    heights_out, flow_out, mech_out, heights, flow, fx, fy, r, rows_in, upper, sem,
):
    depth, width, lanes = pre.shape
    groups = width // 8
    f32 = jnp.float32
    depth_total = depth * counts[2]
    scale = 2.0 / depth_total
    stores = [pltpu.make_async_copy(mech, mech_out, sem.at[0]), pltpu.make_async_copy(heights, heights_out, sem.at[1])]
    stores[0].start()
    lane = lax.broadcasted_iota(jnp.int32, (WIDE, lanes), 1)
    outer = jnp.logical_or(lane == 0, lane == lanes - 1)
    lane8 = lax.broadcasted_iota(jnp.int32, (8, lanes), 1)
    chunks = range(0, width, WIDE)
    far = range(1, counts[2])
    place = lax.axis_index("gz")

    below, above = jnp.zeros((width, lanes), f32), jnp.zeros((width, lanes), f32)
    for off in far:
        piece = cs[off - 1]
        low = (place >= off).astype(f32)
        below = below + piece * low
        above = above + piece * (1.0 - low)
    below = below * (1.0 / depth_total)
    above = scale * above
    upper[...] = above
    for z in range(depth):
        heights[z] = pre[z] * (1.0 / depth_total) + below
    stores[1].start()
    low, high = jnp.zeros((8, lanes), f32), jnp.zeros((8, lanes), f32)
    for g in range(groups):
        values = above[8 * g:8 * g + 8, :]
        low = jnp.where(lane8 == g, pltpu.roll(values, g, 1), low)
        high = jnp.where(lane8 == g, pltpu.roll(values, g + 1, 1), high)
    packed = [low, high]
    for side in (0, 1):
        beyond = jnp.zeros((8, lanes), f32)
        for off in far:
            beyond = beyond + scale * tyr[side, off - 1]
        packed.append(beyond)
    step = groups
    while step < lanes:
        turned = [pltpu.roll(x, step, 1) for x in packed]
        packed = [x + y for x, y in zip(packed, turned)]
        step *= 2
    ends = []
    for side, end in ((0, above[0:1, :]), (1, above[width - 1:width, :])):
        here = (ye[side, 1] + packed[side]) * ye[side, 2]
        there = (yer[side, 1] + packed[2 + side]) * yer[side, 2]
        ends.append(gye[side] / (here + there))
        beyond = jnp.zeros((1, lanes), f32)
        for off in far:
            beyond = beyond + scale * txr[side, off - 1]
        here = (xe[side, 1] + end) * xe[side, 2]
        there = (xer[side, 1] + beyond) * xer[side, 2]
        rows_in[side] = gxe[side] / (here + there)
    odd = lax.rem(lane8, 2) == 1
    first_end = pltpu.roll(ends[0], 1, 1)
    flow_woven = jnp.where(odd, first_end, ends[1]), jnp.where(odd, ends[1], first_end)

    def resist(z, carry):
        r[z, 0:width, :] = part[z] + upper[...] * inv[z]
        return carry

    lax.fori_loop(0, depth + 2, resist, 0, unroll=depth + 2)

    def sides(woven, z, row):
        tiles = []
        for g in range(WIDE // 8):
            slot = z * groups + row // 8 + g
            tiles.append(pltpu.roll(woven[(row // 8 + g) % 2], lanes - 1 - slot, 1))
        return jnp.where(outer, jnp.concatenate(tiles, axis=0), 0.0)

    def rise(z, rows):
        return gz[z, rows, :] / (r[z, rows, :] + r[z + 1, rows, :])

    def lateral(z, carry):
        fx[z, PAD - 1:PAD, :] = rows_in[0, pl.ds(z, 1), :]
        mid = r[z + 1, 0:width, :]
        fy[z] = gy[z] / (mid + pltpu.roll(mid, lanes - 1, 1))
        fx[z, PAD:PAD + width, :] = gx[z] / (mid + r[z + 1, 1:width + 1, :])
        fx[z, PAD + width - 1:PAD + width, :] = rows_in[1, pl.ds(z, 1), :]
        return carry

    def step_z(z, carry):
        out = []
        for row, under in zip(chunks, carry):
            rows = slice(row, row + WIDE)
            over = rise(z + 1, rows)
            face = fy[z, rows, :]
            total = (over - under) + (face - pltpu.roll(face, 1, 1)) - s[z + 1, rows, :]
            total = total + (fx[z, PAD + row:PAD + row + WIDE, :] - fx[z, PAD + row - 1:PAD + row - 1 + WIDE, :])
            flow[z, rows, :] = total + sides(flow_woven, z, row)
            out.append(over)
        return tuple(out)

    carry = tuple(rise(0, slice(row, row + WIDE)) for row in chunks)
    parts = 4 if depth % 4 == 0 else 1
    some = depth // parts
    for n in range(parts):
        span = n * some, (n + 1) * some
        lax.fori_loop(*span, lateral, 0, unroll=some)
        carry = lax.fori_loop(*span, step_z, carry, unroll=some)
        layers = pl.ds(n * some, some)
        pltpu.make_async_copy(flow.at[layers], flow_out.at[layers], sem.at[2]).start()
    pltpu.make_async_copy(flow, flow_out, sem.at[2]).wait()
    for copy in stores:
        copy.wait()


def local(counts, displacement, pressure, zone, perm_table, thickness):
    _, depth, width, lanes = displacement.shape
    f32, i32 = jnp.float32, jnp.int32
    tall = (depth + 2, width + 2 * PAD, lanes)
    cells, plane = (depth, width, lanes), (width, lanes)
    hbm, vmem = (pl.BlockSpec(memory_space=m) for m in (pl.ANY, pltpu.VMEM))
    far = max(counts[2] - 1, 1)
    V = lambda *shape, dtype=f32: pltpu.VMEM(shape, dtype)
    D = pltpu.SemaphoreType.DMA
    inputs = [
        pltpu.with_memory_space_constraint(x, pltpu.HBM)
        for x in (displacement, pressure, zone, perm_table, thickness)
    ]
    layers = (depth + 2, width, lanes)
    rows, packs = (depth, lanes), (8, lanes)
    results = (
        V(*cells), V(far, *plane), V(*layers), V(*layers), V(*cells), V(*cells), V(depth + 1, *plane), V(*layers),
        V(3, *cells), V(2, *rows), V(2, *packs), V(2, 3, *rows), V(2, 3, *rows), V(2, 3, *packs), V(2, 3, *packs),
        V(2, far, 1, lanes), V(2, far, *packs),
    )
    fields = pl.pallas_call(
        functools.partial(kernel, counts),
        out_shape=results,
        in_specs=[hbm] * 5,
        out_specs=(vmem,) * len(results),
        scratch_shapes=[
            V(3, *tall), V(*tall), V(depth, width + 2 * PAD, lanes), V(*layers, dtype=i32), V(*plane, dtype=i32),
            pltpu.SMEM((ZONES,), f32), V(*cells), V(*plane), V(2, 4, *rows), V(2, 4, *rows), V(2, 4, *packs), V(2, 4, *packs),
            V(2, *rows, dtype=i32), V(2, *packs, dtype=i32), V(2, 1, lanes), V(2, *packs),
            V(2 * far, 1, lanes), V(2 * far, *packs), D((7,)), D((9,)), D((3,)), D((1,)), D((1,)), D((2,)), D((2,)),
        ],
        compiler_params=pltpu.CompilerParams(
            collective_id=0, has_side_effects=True, vmem_limit_bytes=40 * 2**20
        ),
    )(*inputs)
    return pl.pallas_call(
        functools.partial(finish, counts),
        out_shape=tuple(jax.ShapeDtypeStruct(x.shape, f32) for x in (pressure, pressure, displacement)),
        in_specs=[vmem] * len(results),
        out_specs=(hbm,) * 3,
        scratch_shapes=[
            V(*cells), V(*cells), V(depth, width + 2 * PAD, lanes), V(*cells), V(depth + 2, width + 8, lanes),
            V(2, *rows), V(*plane), D((3,)),
        ],
        compiler_params=pltpu.CompilerParams(vmem_limit_bytes=8 * 2**20),
    )(*[pltpu.with_memory_space_constraint(x, pltpu.VMEM) for x in fields])


def solution(mesh):
    counts = tuple(mesh.shape[axis] for axis in AXES)
    in_specs = (
        P(None, "gz", "gx", "gy"),
        P("gz", "gx", "gy"),
        P("gz", "gx", "gy"),
        P(),
        P("gx", "gy"),
    )
    out_specs = (P("gz", "gx", "gy"), P("gz", "gx", "gy"), P(None, "gz", "gx", "gy"))
    return jax.shard_map(
        functools.partial(local, counts), mesh=mesh, in_specs=in_specs, out_specs=out_specs, check_vma=False
    )
```

```python
import functools

import jax
import jax.numpy as jnp
from jax import lax
from jax.experimental import pallas as pl
from jax.experimental.pallas import tpu as pltpu
from jax.sharding import PartitionSpec as P

MESH = pl.DeviceIdType.MESH
ZONES = 8
AXES = ("gx", "gy", "gz")
PAD = 8
ROWS = 32
WIDE = 64

ZU, ZB, X0, Y0, X1, Y1, ZS, X2, Y2 = range(9)


def kernel(
    counts, disp, press, zone, table, thick,
    pre, cs, r, inv, gx, gy, gz, s, mech, gxe, gye, xe, xer, ye, yer, txr, tyr,
    u, p, t, zn, th, tab, ip, tot, xs, xr, ys, yr, zr, zp, tx, ty, tall_x, tall_y,
    load_sem, recv_sem, side_send, col_send, col_recv, edge_send, edge_recv,
):
    depth, width, lanes = press.shape
    groups = width // 8
    last = PAD + width
    me = {axis: lax.axis_index(axis) for axis in AXES}
    size = dict(zip(AXES, counts))
    depth_total = depth * size["gz"]
    scale = 2.0 / depth_total
    own = pl.ds(PAD, width)
    f32 = jnp.float32
    chunks = range(0, width, ROWS)
    far = range(1, size["gz"])

    def has(axis, side):
        return me[axis] > 0 if side == 0 else me[axis] < size[axis] - 1

    def mask(axis, side):
        return has(axis, side).astype(f32)

    def peer(axis, side, up=None):
        place = {axis: me[axis] + (1 if side else -1)}
        if up is not None:
            place["gz"] = me["gz"] + up
        return place

    def round_z(off):
        return {"gz": lax.rem(me["gz"] + off, size["gz"])}

    def both(axis, side, off):
        inside = me["gz"] + off < size["gz"] if off > 0 else me["gz"] + off >= 0
        return jnp.logical_and(has(axis, side), inside)

    def loop(step, carry, start=0, end=depth):
        return lax.fori_loop(start, end, step, carry, unroll=end - start)

    inner = pl.ds(1, depth)
    loads = [
        pltpu.make_async_copy(disp.at[1], u.at[1, inner, own], load_sem.at[0]),
        pltpu.make_async_copy(disp.at[0], u.at[0, inner, own], load_sem.at[1]),
        pltpu.make_async_copy(disp.at[2], u.at[2, inner, own], load_sem.at[2]),
        pltpu.make_async_copy(press, p.at[inner, own], load_sem.at[3]),
        pltpu.make_async_copy(zone, zn.at[inner], load_sem.at[4]),
        pltpu.make_async_copy(thick, th, load_sem.at[5]),
        pltpu.make_async_copy(table, tab, load_sem.at[6]),
    ]
    loads[0].start()

    barrier = pltpu.get_barrier_semaphore()
    partners = jnp.int32(size["gz"] - 1)
    for axis in ("gx", "gy"):
        for side in (0, 1):
            @pl.when(has(axis, side))
            def _():
                pl.semaphore_signal(barrier, inc=1, device_id=peer(axis, side), device_id_type=MESH)
            partners = partners + has(axis, side).astype(jnp.int32) * (1 + me["gz"])
    for off in far:
        pl.semaphore_signal(barrier, inc=1, device_id=round_z(off), device_id_type=MESH)
    for load in loads[1:]:
        load.start()
    for axis in ("gx", "gy"):
        for side in (0, 1):
            for off in far:
                @pl.when(both(axis, side, off))
                def _():
                    pl.semaphore_signal(barrier, inc=1, device_id=peer(axis, side, off), device_id_type=MESH)

    def copy(message, axis, side, src, dst, at):
        return pltpu.make_async_remote_copy(
            src_ref=src,
            dst_ref=dst,
            send_sem=side_send.at[AXES.index(axis)],
            recv_sem=recv_sem.at[message],
            device_id=peer(axis, at),
            device_id_type=MESH,
        )

    def send(message, axis, *parts):
        for side in (0, 1):
            @pl.when(has(axis, side))
            def _():
                for srcs, dsts in parts:
                    copy(message, axis, side, srcs[side], dsts[1 - side], side).start()

    def sides_of(axis):
        return has(axis, 0).astype(jnp.int32) + has(axis, 1).astype(jnp.int32)

    def finished(sem, axis, part):
        for n in (1, 2):
            @pl.when(sides_of(axis) == n)
            def _():
                pltpu.make_async_copy(part(n), part(n), sem).wait()

    def receive(message, axis, part):
        finished(recv_sem.at[message], axis, part)

    def clear(axis, refs):
        for side in (0, 1):
            @pl.when(jnp.logical_not(has(axis, side)))
            def _():
                for ref in refs[side]:
                    ref[...] = jnp.zeros(ref.shape, ref.dtype)

    def pair(ref, *at):
        return (ref.at[(0, *at)], ref.at[(1, *at)])

    zu = ((u.at[2, 1, own], u.at[2, depth, own]), (u.at[2, 0, own], u.at[2, depth + 1, own]))
    zl = (
        (disp.at[pl.ds(0, 2), 0], disp.at[pl.ds(0, 2), depth - 1]),
        (u.at[pl.ds(0, 2), 0, own], u.at[pl.ds(0, 2), depth + 1, own]),
    )
    zq = ((press.at[0], press.at[depth - 1]), (p.at[0, own], p.at[depth + 1, own]))
    zz = ((zone.at[0], zone.at[depth - 1]), (zn.at[0], zn.at[depth + 1]))
    zs = ((s.at[1], s.at[depth]), (s.at[0], s.at[depth + 1]))
    x0, y0 = (pair(xs, 0), pair(xr, 0)), (pair(ys, 0), pair(yr, 0))
    x1, y1 = (pair(xs, pl.ds(1, 3)), pair(xr, pl.ds(1, 3))), (pair(ys, pl.ds(1, 3)), pair(yr, pl.ds(1, 3)))
    x2, y2 = (pair(xe), pair(xer)), (pair(ye), pair(yer))

    lane = lax.broadcasted_iota(jnp.int32, (8, lanes), 1)
    odd = lax.rem(lane, 2) == 1
    lane_r = lax.broadcasted_iota(jnp.int32, (ROWS, lanes), 1)
    first_lane, last_lane = lane_r == 0, lane_r == lanes - 1
    outer_lane = jnp.logical_or(first_lane, last_lane)
    zero8 = jnp.zeros((8, lanes), f32)

    def pack(values, slot, packs):
        turned = pltpu.roll(values, slot, 1)
        low = jnp.where(lane == slot, turned, packs[0])
        return low, jnp.where(lane == lax.rem(slot + lanes - 1, lanes), turned, packs[1])

    def keep(ref, packs, *at):
        ref[(0, *at)] = packs[0]
        ref[(1, *at)] = pltpu.roll(packs[1], 1, 1)

    def pack_rows(values, z, row, packs):
        for g in range(values.shape[0] // 8):
            packs = pack(values[8 * g:8 * g + 8, :], z * groups + row // 8 + g, packs)
        return packs

    def weave(low, high):
        low = pltpu.roll(low, 1, 1)
        return jnp.where(odd, low, high), jnp.where(odd, high, low)

    def ends_at(woven, z, row):
        parts = []
        for g in range(ROWS // 8):
            slot = z * groups + row // 8 + g
            parts.append(pltpu.roll(woven[(row // 8 + g) % 2], lanes - 1 - slot, 1))
        return jnp.concatenate(parts, axis=0)

    def yshift(v, ends):
        below, above = pltpu.roll(v, 1, 1), pltpu.roll(v, lanes - 1, 1)
        return jnp.where(first_lane, ends, below), jnp.where(last_lane, ends, above)

    fields = [u.at[0], u.at[1], u.at[2], p]

    def pack_field(i, n):
        def step(z, packs):
            return pack_rows(fields[i][z + 1, PAD:last, :], z, 0, packs)

        keep(ys, loop(step, (zero8, zero8)), n)

    def take_rows(i):
        def step(z, carry):
            xs[0, i, pl.ds(z, 1), :] = fields[i][z + 1, PAD:PAD + 1, :]
            xs[1, i, pl.ds(z, 1), :] = fields[i][z + 1, last - 1:last, :]
            return carry

        loop(step, 0)

    loads[0].wait()
    pack_field(1, 0)
    loads[1].wait()
    take_rows(0)
    loads[2].wait()
    pl.semaphore_wait(barrier, partners)
    send(ZU, "gz", zu)
    send(X0, "gx", x0)
    send(Y0, "gy", y0)
    send(ZB, "gz", zl, zq, zz)

    loads[3].wait()
    for i in range(1, 4):
        take_rows(i)
    pack_field(0, 1)
    pack_field(2, 2)
    pack_field(3, 3)
    send(X1, "gx", x1)
    send(Y1, "gy", y1)

    clear("gx", [[ref.at[side] for ref in (xr, xer)] for side in (0, 1)])
    clear("gy", [[ref.at[side] for ref in (yr, yer)] for side in (0, 1)])
    edges = (0, depth + 1)
    clear("gz", [[u.at[:, z, own], p.at[z, own], s.at[z], zn.at[z]] for z in edges])
    for axis, ref in (("gx", txr), ("gy", tyr)):
        for side in (0, 1):
            for off in far:
                @pl.when(jnp.logical_not(both(axis, side, off)))
                def _():
                    ref[side, off - 1] = jnp.zeros(ref.shape[2:], f32)

    for load in loads[4:]:
        load.wait()
    base = me["gz"] * depth

    inverse = [1.0 / jnp.full((8, lanes), tab[i], f32) for i in range(ZONES)]

    def rows_resistance(zones, active):
        count = zones.shape[0] // 8
        least = jnp.concatenate([inverse[0]] * count, axis=0)
        for i in range(1, ZONES):
            least = jnp.where(zones == i, jnp.concatenate([inverse[i]] * count, axis=0), least)
        return jnp.where(active, least * (1.0 / (0.001 + 0.999)), least * (1.0 / 0.001))

    def zone_step(z, packs):
        for row in chunks:
            zones = zn[z + 1, row:row + ROWS, :]
            ip[z, row:row + ROWS, :] = rows_resistance(zones, base + z < th[row:row + ROWS, :])
            packs = pack_rows(zones, z, row, packs)
        zr[0, pl.ds(z, 1), :] = zn[z + 1, 0:1, :]
        zr[1, pl.ds(z, 1), :] = zn[z + 1, width - 1:width, :]
        return packs

    none8 = jnp.zeros((8, lanes), jnp.int32)
    keep(zp, loop(zone_step, (none8, none8)))

    def spread(packs):
        step = groups
        while step < lanes:
            turned = [pltpu.roll(x, step, 1) for x in packs]
            packs = [x + y for x, y in zip(packs, turned)]
            step *= 2
        return packs

    edge_height = pack_rows(th[...], 0, 0, (none8, none8))
    edge_height = spread([edge_height[0], pltpu.roll(edge_height[1], 1, 1)])
    edge_layer = base + lane // groups

    for row in chunks:
        rows = slice(row, row + ROWS)
        at = slice(PAD + row, PAD + row + ROWS)

        def partial_step(z, carry, bottom=False, top=False):
            v = u[1, z + 1, at, :]
            ym, yp = pltpu.roll(v, 1, 1), pltpu.roll(v, lanes - 1, 1)
            div = jnp.where(last_lane, 0.0, yp) - jnp.where(first_lane, 0.0, ym)
            if not top:
                div = div + u[2, z + 2, at, :]
            if not bottom:
                div = div - u[2, z, at, :]
            t[z, at, :] = div
            return carry

        partial_step(0, 0, bottom=True)
        loop(partial_step, 0, 1, depth - 1)
        partial_step(depth - 1, 0, top=True)

    receive(ZU, "gz", lambda n: ip.at[pl.ds(0, n)])
    receive(X0, "gx", lambda n: xr.at[pl.ds(0, n), 0])
    receive(Y0, "gy", lambda n: yr.at[pl.ds(0, n), 0])

    def unpack_first(z, carry):
        u[0, z + 1, PAD - 1:PAD, :] = xr[0, 0, pl.ds(z, 1), :]
        u[0, z + 1, last:last + 1, :] = xr[1, 0, pl.ds(z, 1), :]
        return carry

    loop(unpack_first, 0)

    woven = weave(-yr[0, 0], yr[1, 0])

    def strain_of(z, row, bottom=False, top=False):
        at = slice(PAD + row, PAD + row + ROWS)
        up = u[0, z + 1, PAD + row + 1:PAD + row + 1 + ROWS, :]
        down = u[0, z + 1, PAD + row - 1:PAD + row - 1 + ROWS, :]
        div = t[z, at, :] + (up - down) + jnp.where(outer_lane, ends_at(woven, z, row), 0.0)
        if bottom:
            div = div - u[2, 0, at, :]
        if top:
            div = div + u[2, depth + 1, at, :]
        return 0.3 * jnp.tanh(0.5 * div)

    for row in chunks:
        rows = slice(row, row + ROWS)
        height = th[rows, :]

        def strain_step(z, acc, bottom=False, top=False):
            st = strain_of(z, row, bottom, top)
            s[z + 1, rows, :] = st
            acc = acc + jnp.where(base + z < height, 1.0 + st, 0.0)
            pre[z, rows, :] = acc
            return acc

        acc = strain_step(0, jnp.zeros((ROWS, lanes), f32), bottom=True)
        acc = loop(strain_step, acc, 1, depth - 1)
        tot[rows, :] = strain_step(depth - 1, acc, top=True)

    def column(off, at):
        return pltpu.make_async_remote_copy(
            src_ref=tot,
            dst_ref=cs.at[off - 1],
            send_sem=col_send.at[0],
            recv_sem=col_recv.at[0],
            device_id=round_z(at),
            device_id_type=MESH,
        )

    for side, row in ((0, 0), (1, width - 1)):
        tx[side] = tot[row:row + 1, :]
    keep(ty, pack_rows(tot[...], 0, 0, (zero8, zero8)))

    def edge_wait(sems, places):
        for i, (axis, ref) in enumerate((("gx", tall_x), ("gy", tall_y))):
            for n in sorted({a * b for a in (1, 2) for b in far}):
                @pl.when(sides_of(axis) * places == n)
                def _():
                    some = ref.at[pl.ds(0, n)]
                    pltpu.make_async_copy(some, some, sems.at[i]).wait()

    def start_edges(n):
        off = me["gz"] - n
        for i, (axis, src, dst) in enumerate((("gx", tx, txr), ("gy", ty, tyr))):
            for side in (0, 1):
                @pl.when(jnp.logical_and(has(axis, side), off > 0))
                def _():
                    pltpu.make_async_remote_copy(
                        src_ref=src.at[side],
                        dst_ref=dst.at[1 - side, off - 1],
                        send_sem=edge_send.at[i],
                        recv_sem=edge_recv.at[i],
                        device_id=peer(axis, side, -off),
                        device_id_type=MESH,
                    ).start()

    def start_column(n):
        target = n + (n >= me["gz"]).astype(jnp.int32)
        ahead = lax.rem(target - me["gz"] + size["gz"], size["gz"])
        column(ahead, ahead).start()

    if far:
        for n in far:
            start_edges(n - 1)
        start_column(0)

    packs = loop(lambda z, packs: pack_rows(s[z + 1], z, 0, packs), (zero8, zero8))
    edge = packs[0], pltpu.roll(packs[1], 1, 1)
    actives = [edge_layer < edge_height[side] for side in (0, 1)]
    thicknesses = [jnp.where(actives[side], 1.0 + edge[side], 0.0) for side in (0, 1)]
    aboves, step = thicknesses, groups
    while step < lanes:
        turned = [pltpu.roll(x, lanes - step, 1) for x in aboves]
        aboves = [x + jnp.where(lane < lanes - step, y, 0.0) for x, y in zip(aboves, turned)]
        step *= 2
    for side in (0, 1):
        st, active, thickness = edge[side], actives[side], thicknesses[side]
        h = 1.0 + st
        ye[side, 0] = st
        ye[side, 1] = 1.0 + scale * (aboves[side] - thickness)
        ye[side, 2] = rows_resistance(zp[side], active) / (h * h * h)
        row = (width - 1) * side

        def row_step(z, carry):
            xe[side, 0, pl.ds(z, 1), :] = s[z + 1, row:row + 1, :]
            xe[side, 1, pl.ds(z, 1), :] = 1.0 + scale * (tot[row:row + 1, :] - pre[z, row:row + 1, :])
            return carry

        loop(row_step, 0)
        h = 1.0 + xe[side, 0]
        layer = base + lax.broadcasted_iota(jnp.int32, (depth, lanes), 0)
        xe[side, 2] = rows_resistance(zr[side], layer < th[row:row + 1, :]) / (h * h * h)

    send(X2, "gx", x2)
    send(Y2, "gy", y2)
    for n in far[1:]:
        start_column(n - 1)
    send(ZS, "gz", zs)

    receive(X1, "gx", lambda n: xr.at[pl.ds(0, n), pl.ds(1, 3)])
    receive(Y1, "gy", lambda n: yr.at[pl.ds(0, n), pl.ds(1, 3)])

    def gradient_step(z, carry):
        t[z, PAD:last, :] = 0.25 * s[z + 1] - 0.5 * p[z + 1, PAD:last, :]
        return carry

    loop(gradient_step, 0)

    def unpack_inputs(z, carry):
        for side, at in ((0, PAD - 1), (1, last)):
            for i in (1, 2):
                fields[i][z + 1, at:at + 1, :] = xr[side, i, pl.ds(z, 1), :]
            t[z, at:at + 1, :] = -0.5 * xr[side, 3, pl.ds(z, 1), :]
        return carry

    loop(unpack_inputs, 0)

    wovens = [weave(yr[0, n], yr[1, n]) for n in (1, 0, 2)]
    for row in chunks:
        rows = slice(row, row + ROWS)
        at = slice(PAD + row, PAD + row + ROWS)
        up1 = slice(PAD + row + 1, PAD + row + 1 + ROWS)
        down1 = slice(PAD + row - 1, PAD + row - 1 + ROWS)
        height = tot[rows, :]

        def inner_step(z, below, bottom=False, top=False):
            mids = [u[c, z + 1, at, :] for c in range(3)]
            pm, st, tm = p[z + 1, at, :], s[z + 1, rows, :], t[z, at, :]
            above = None
            if not top:
                twice = 2.0 / (2.0 + st + s[z + 2, rows, :])
                above = [twice * (u[c, z + 2, at, :] - mids[c]) for c in range(3)]
                gz[z + 1, rows, :] = 2.0 * twice * (p[z + 2, at, :] - pm)
            tb, ta = pltpu.roll(tm, 1, 1), pltpu.roll(tm, lanes - 1, 1)
            grads = [
                t[z, up1, :] - t[z, down1, :],
                jnp.where(last_lane, 0.0, ta) - jnp.where(first_lane, 0.0, tb),
            ]
            if bottom:
                grads.append(t[z + 1, at, :])
            elif top:
                grads.append(-t[z - 1, at, :])
            else:
                grads.append(t[z + 1, at, :] - t[z - 1, at, :])
            for c in range(3):
                ym, yp = yshift(mids[c], ends_at(wovens[c], z, row))
                out = u[c, z + 1, up1, :] + u[c, z + 1, down1, :] + ym + yp - 4.0 * mids[c] + grads[c]
                if not top:
                    out = out + above[c]
                if not bottom:
                    out = out - below[c]
                mech[c, z, rows, :] = out
            gx[z, rows, :] = 2.0 * (p[z + 1, up1, :] - pm)
            gy[z, rows, :] = jnp.where(last_lane, 0.0, 2.0 * (pltpu.roll(pm, lanes - 1, 1) - pm))
            h = 1.0 + st
            free = ip[z, rows, :] / (h * h * h)
            inv[z + 1, rows, :] = free
            r[z + 1, rows, :] = free + (scale * (height - pre[z, rows, :])) * free
            return tuple(above) if above else None

        below = inner_step(0, None, bottom=True)
        below = loop(lambda z, b: inner_step(z, b), below, 1, depth - 1)
        inner_step(depth - 1, below, top=True)

    receive(ZB, "gz", lambda n: ip.at[pl.ds(0, 4 * n)])
    receive(ZS, "gz", lambda n: ip.at[pl.ds(0, n)])

    for row in chunks:
        rows = slice(row, row + ROWS)
        at = slice(PAD + row, PAD + row + ROWS)
        for side, z, halo in ((0, 0, 0), (1, depth - 1, depth + 1)):
            sign = 1.0 if side else -1.0
            st = s[halo, rows, :]
            twice = 2.0 / (2.0 + s[z + 1, rows, :] + st)
            for c in range(3):
                out = mech[c, z, rows, :] + twice * (u[c, halo, at, :] - u[c, z + 1, at, :])
                if c == 2:
                    out = out + sign * (0.25 * st - 0.5 * p[halo, at, :])
                mech[c, z, rows, :] = out
            gz[z + side, rows, :] = (2.0 * sign * mask("gz", side)) * (twice * (p[halo, at, :] - p[z + 1, at, :]))
            active = base + halo - 1 < th[rows, :]
            h = 1.0 + st
            free = rows_resistance(zn[halo, rows, :], active) / (h * h * h)
            part = jnp.where(active, -h, 0.0) if side else tot[rows, :]
            r[halo, rows, :] = free + (scale * part) * free
            inv[halo, rows, :] = free

    receive(X2, "gx", lambda n: xer.at[pl.ds(0, n)])
    receive(Y2, "gy", lambda n: yer.at[pl.ds(0, n)])

    def side_rows(z, carry):
        for side, x in ((0, 0), (1, width - 1)):
            step = (0.25 if side else -0.25) * xer[side, 0, pl.ds(z, 1), :]
            mech[0, z, x:x + 1, :] = mech[0, z, x:x + 1, :] + step
        return carry

    loop(side_rows, 0)
    for side in (0, 1):
        sign = 1.0 if side else -1.0
        gxe[side] = (2.0 * sign * mask("gx", side)) * (xr[side, 3] - xs[side, 3])
        gye[side] = (2.0 * mask("gy", side)) * (yr[side, 3] - ys[side, 3])
    woven = weave(-(0.25 * yer[0, 0] - 0.5 * yr[0, 3]), 0.25 * yer[1, 0] - 0.5 * yr[1, 3])

    def side_lanes(z, carry):
        for row in chunks:
            rows = slice(row, row + ROWS)
            mech[1, z, rows, :] = mech[1, z, rows, :] + jnp.where(outer_lane, ends_at(woven, z, row), 0.0)
        return carry

    loop(side_lanes, 0)

    every = ip.at[pl.ds(0, size["gz"] - 1)]
    pltpu.make_async_copy(every, every, col_recv.at[0]).wait()
    edge_wait(edge_recv, size["gz"] - 1 - me["gz"])

    finished(side_send.at[0], "gx", lambda n: inv.at[pl.ds(0, 7 * n), pl.ds(0, depth)])
    finished(side_send.at[1], "gy", lambda n: inv.at[pl.ds(0, 7 * n), pl.ds(0, 8)])
    finished(side_send.at[2], "gz", lambda n: inv.at[pl.ds(0, 6 * n)])
    pltpu.make_async_copy(every, every, col_send.at[0]).wait()
    edge_wait(edge_send, me["gz"])


def finish(
    counts, pre, cs, part, inv, gx, gy, gz, s, mech, gxe, gye, xe, xer, ye, yer, txr, tyr,
    heights_out, flow_out, mech_out, heights, flow, fx, fy, r, rows_in, upper, sem,
):
    depth, width, lanes = pre.shape
    groups = width // 8
    f32 = jnp.float32
    depth_total = depth * counts[2]
    scale = 2.0 / depth_total
    stores = [pltpu.make_async_copy(mech, mech_out, sem.at[0]), pltpu.make_async_copy(heights, heights_out, sem.at[1])]
    stores[0].start()
    lane = lax.broadcasted_iota(jnp.int32, (WIDE, lanes), 1)
    outer = jnp.logical_or(lane == 0, lane == lanes - 1)
    lane8 = lax.broadcasted_iota(jnp.int32, (8, lanes), 1)
    chunks = range(0, width, WIDE)
    far = range(1, counts[2])
    place = lax.axis_index("gz")

    below, above = jnp.zeros((width, lanes), f32), jnp.zeros((width, lanes), f32)
    for off in far:
        piece = cs[off - 1]
        low = (place >= off).astype(f32)
        below = below + piece * low
        above = above + piece * (1.0 - low)
    below = below * (1.0 / depth_total)
    above = scale * above
    upper[...] = above
    for z in range(depth):
        heights[z] = pre[z] * (1.0 / depth_total) + below
    stores[1].start()
    low, high = jnp.zeros((8, lanes), f32), jnp.zeros((8, lanes), f32)
    for g in range(groups):
        values = above[8 * g:8 * g + 8, :]
        low = jnp.where(lane8 == g, pltpu.roll(values, g, 1), low)
        high = jnp.where(lane8 == g, pltpu.roll(values, g + 1, 1), high)
    packed = [low, high]
    for side in (0, 1):
        beyond = jnp.zeros((8, lanes), f32)
        for off in far:
            beyond = beyond + scale * tyr[side, off - 1]
        packed.append(beyond)
    step = groups
    while step < lanes:
        turned = [pltpu.roll(x, step, 1) for x in packed]
        packed = [x + y for x, y in zip(packed, turned)]
        step *= 2
    ends = []
    for side, end in ((0, above[0:1, :]), (1, above[width - 1:width, :])):
        here = (ye[side, 1] + packed[side]) * ye[side, 2]
        there = (yer[side, 1] + packed[2 + side]) * yer[side, 2]
        ends.append(gye[side] / (here + there))
        beyond = jnp.zeros((1, lanes), f32)
        for off in far:
            beyond = beyond + scale * txr[side, off - 1]
        here = (xe[side, 1] + end) * xe[side, 2]
        there = (xer[side, 1] + beyond) * xer[side, 2]
        rows_in[side] = gxe[side] / (here + there)
    odd = lax.rem(lane8, 2) == 1
    first_end = pltpu.roll(ends[0], 1, 1)
    flow_woven = jnp.where(odd, first_end, ends[1]), jnp.where(odd, ends[1], first_end)

    def resist(z, carry):
        r[z, 0:width, :] = part[z] + upper[...] * inv[z]
        return carry

    lax.fori_loop(0, 2, resist, 0, unroll=2)

    def sides(woven, z, row):
        tiles = []
        for g in range(WIDE // 8):
            slot = z * groups + row // 8 + g
            tiles.append(pltpu.roll(woven[(row // 8 + g) % 2], lanes - 1 - slot, 1))
        return jnp.where(outer, jnp.concatenate(tiles, axis=0), 0.0)

    def rise(z, rows):
        return gz[z, rows, :] / (r[z, rows, :] + r[z + 1, rows, :])

    def lateral(z, carry):
        fx[z, PAD - 1:PAD, :] = rows_in[0, pl.ds(z, 1), :]
        mid = r[z + 1, 0:width, :]
        fy[z] = gy[z] / (mid + pltpu.roll(mid, lanes - 1, 1))
        fx[z, PAD:PAD + width, :] = gx[z] / (mid + r[z + 1, 1:width + 1, :])
        fx[z, PAD + width - 1:PAD + width, :] = rows_in[1, pl.ds(z, 1), :]
        return carry

    def step_z(z, carry):
        out = []
        for row, under in zip(chunks, carry):
            rows = slice(row, row + WIDE)
            over = rise(z + 1, rows)
            face = fy[z, rows, :]
            total = (over - under) + (face - pltpu.roll(face, 1, 1)) - s[z + 1, rows, :]
            total = total + (fx[z, PAD + row:PAD + row + WIDE, :] - fx[z, PAD + row - 1:PAD + row - 1 + WIDE, :])
            flow[z, rows, :] = total + sides(flow_woven, z, row)
            out.append(over)
        return tuple(out)

    carry = tuple(rise(0, slice(row, row + WIDE)) for row in chunks)
    parts = 4 if depth % 4 == 0 else 1
    some = depth // parts
    for n in range(parts):
        span = n * some, (n + 1) * some
        lax.fori_loop(n * some + 2, (n + 1) * some + 2, resist, 0, unroll=some)
        lax.fori_loop(*span, lateral, 0, unroll=some)
        carry = lax.fori_loop(*span, step_z, carry, unroll=some)
        layers = pl.ds(n * some, some)
        pltpu.make_async_copy(flow.at[layers], flow_out.at[layers], sem.at[2]).start()
    pltpu.make_async_copy(flow, flow_out, sem.at[2]).wait()
    for copy in stores:
        copy.wait()


def local(counts, displacement, pressure, zone, perm_table, thickness):
    _, depth, width, lanes = displacement.shape
    f32, i32 = jnp.float32, jnp.int32
    tall = (depth + 2, width + 2 * PAD, lanes)
    cells, plane = (depth, width, lanes), (width, lanes)
    hbm, vmem = (pl.BlockSpec(memory_space=m) for m in (pl.ANY, pltpu.VMEM))
    far = max(counts[2] - 1, 1)
    V = lambda *shape, dtype=f32: pltpu.VMEM(shape, dtype)
    D = pltpu.SemaphoreType.DMA
    inputs = [
        pltpu.with_memory_space_constraint(x, pltpu.HBM)
        for x in (displacement, pressure, zone, perm_table, thickness)
    ]
    layers = (depth + 2, width, lanes)
    rows, packs = (depth, lanes), (8, lanes)
    results = (
        V(*cells), V(far, *plane), V(*layers), V(*layers), V(*cells), V(*cells), V(depth + 1, *plane), V(*layers),
        V(3, *cells), V(2, *rows), V(2, *packs), V(2, 3, *rows), V(2, 3, *rows), V(2, 3, *packs), V(2, 3, *packs),
        V(2, far, 1, lanes), V(2, far, *packs),
    )
    fields = pl.pallas_call(
        functools.partial(kernel, counts),
        out_shape=results,
        in_specs=[hbm] * 5,
        out_specs=(vmem,) * len(results),
        scratch_shapes=[
            V(3, *tall), V(*tall), V(depth, width + 2 * PAD, lanes), V(*layers, dtype=i32), V(*plane, dtype=i32),
            pltpu.SMEM((ZONES,), f32), V(*cells), V(*plane), V(2, 4, *rows), V(2, 4, *rows), V(2, 4, *packs), V(2, 4, *packs),
            V(2, *rows, dtype=i32), V(2, *packs, dtype=i32), V(2, 1, lanes), V(2, *packs),
            V(2 * far, 1, lanes), V(2 * far, *packs), D((7,)), D((9,)), D((3,)), D((1,)), D((1,)), D((2,)), D((2,)),
        ],
        compiler_params=pltpu.CompilerParams(
            collective_id=0, has_side_effects=True, vmem_limit_bytes=40 * 2**20
        ),
    )(*inputs)
    return pl.pallas_call(
        functools.partial(finish, counts),
        out_shape=tuple(jax.ShapeDtypeStruct(x.shape, f32) for x in (pressure, pressure, displacement)),
        in_specs=[vmem] * len(results),
        out_specs=(hbm,) * 3,
        scratch_shapes=[
            V(*cells), V(*cells), V(depth, width + 2 * PAD, lanes), V(*cells), V(depth + 2, width + 8, lanes),
            V(2, *rows), V(*plane), D((3,)),
        ],
        compiler_params=pltpu.CompilerParams(vmem_limit_bytes=8 * 2**20),
    )(*[pltpu.with_memory_space_constraint(x, pltpu.VMEM) for x in fields])


def solution(mesh):
    counts = tuple(mesh.shape[axis] for axis in AXES)
    in_specs = (
        P(None, "gz", "gx", "gy"),
        P("gz", "gx", "gy"),
        P("gz", "gx", "gy"),
        P(),
        P("gx", "gy"),
    )
    out_specs = (P("gz", "gx", "gy"), P("gz", "gx", "gy"), P(None, "gz", "gx", "gy"))
    return jax.shard_map(
        functools.partial(local, counts), mesh=mesh, in_specs=in_specs, out_specs=out_specs, check_vma=False
    )
```
